32 devices in a mesh: space: 8 (over z, y), chan: 4 (over x, core).
Axes of the slice: x: 2, y: 2, z: 4, core: 2. Of those that a mesh axis runs over, the one named last changes fastest.
Arguments:
- features: bfloat16 [128, 64, 128], P('space'), may hold values from -6 to 6
- neighbours: int32 [128, 26], P('space'), may hold values from -1 to 127, as said below
- parent_index: int32 [128], P('space'), may hold values from 0 to 31, as said below
- octant: int32 [128], P('space'), may hold values from 0 to 7, as said below
- parent_dest: int32 [32], P('space'), may hold values from 0 to 63, as said below
- conv_fine: bfloat16 [128, 3456], P('chan'), may hold values from -0.109375 to 0.109375
- conv_down: bfloat16 [256, 3456], P('chan'), may hold values from -0.15625 to 0.15625
- conv_coarse: bfloat16 [256, 6912], P('chan'), may hold values from -0.15625 to 0.15625
- norm_gain: float32 [256], P('chan'), may hold values from 0.25 to 1.75
Outputs:
- coarse_parents: bfloat16 [256, 4096], P('chan', 'space')
The draws below stay inside these ranges and needn't reach their ends.
Inputs may be any that keep to these rules, and one draw needn't show every extreme that they name: Brick n lies on device n // 16 of space. Device d holds 16 distinct positions of a slab of 2 x 4 x 4 brick positions (x = 2 d or 2 d + 1, y, z); brick n's position gives parent_index[n] = d * 4 + (y // 2) * 2 + z // 2 and octant[n] = x % 2 + 2 (y % 2) + 4 (z % 2). neighbours[n, k] is the brick at the k-th offset (a, b, c), a, b, c in -1, 0, 1, (0, 0, 0) left out, in increasing 9 a + 3 b + c, or -1 where that position holds no brick. `parent_index`: as stated for neighbours. `octant`: as stated for neighbours. parent_dest[g] = owner * 8 + slot, where the owner of a parent of device d is d - 1, d or d + 1. At most 2 parents of one device go to each of its two neighbours, and some device sends 2 to a neighbour; some owner receives 8 parents. An owner's slots are filled from 0 upward without gaps, in order of source device and then of parent.
All inputs are finite; a program needn't handle non-finite values.
Results may differ from the reference program's by a relative error of at most 0.0065.
Values may be sent and summed in bfloat16 or wider, within the bound.
A program may use at most 64 MiB of HBM per device.

```python
import jax
import jax.numpy as jnp
from jax import lax

FINE_CH = 128
COARSE_CH = 256
EDGE = 4
SLAB_Y = 4
SLAB_Z = 4
BRICK_DEV = 16
PARENT_DEV = 4
SLOTS_DEV = 8
BRICKS = 128
N_SPACE = 8


offset_list = [(a, b, c) for a in (-1, 0, 1) for b in (-1, 0, 1) for c in (-1, 0, 1)]


around_list = [item for item in offset_list if item != (0, 0, 0)]


def geometry(key):
    devices = N_SPACE
    places = 2 * SLAB_Y * SLAB_Z
    keys = jax.random.split(jax.random.fold_in(key, 17), devices)
    chosen = jax.vmap(lambda subkey: jax.random.permutation(subkey, places)[:BRICK_DEV])(keys).astype(jnp.int32)
    device_ids = jnp.arange(devices, dtype=jnp.int32)[:, None] * jnp.ones((1, BRICK_DEV), jnp.int32)
    x_all = 2 * device_ids + chosen % 2
    y_all = chosen // 2 % SLAB_Y
    z_all = chosen // (2 * SLAB_Y)
    width_x = 2 * devices
    brick_ids = jnp.arange(devices * BRICK_DEV, dtype=jnp.int32)
    lookup = jnp.full((width_x * SLAB_Y * SLAB_Z,), -1, jnp.int32)
    flat_pos = (x_all + width_x * (y_all + SLAB_Y * z_all)).reshape(-1)
    lookup = lookup.at[flat_pos].set(brick_ids)
    x_flat = x_all.reshape(-1)
    y_flat = y_all.reshape(-1)
    z_flat = z_all.reshape(-1)
    columns = []
    for a, b, c in around_list:
        next_x = x_flat + a
        next_y = y_flat + b
        next_z = z_flat + c
        inside = (next_x >= 0) & (next_x < width_x) & (next_y >= 0) & (next_y < SLAB_Y) & (next_z >= 0) & (next_z < SLAB_Z)
        spot_index = jnp.where(inside, next_x + width_x * (next_y + SLAB_Y * next_z), 0)
        columns.append(jnp.where(inside, lookup[spot_index], -1))
    neighbour_table = jnp.stack(columns, 1).astype(jnp.int32)
    parent_ids = device_ids * PARENT_DEV + y_all // 2 * (SLAB_Z // 2) + z_all // 2
    octant_ids = chosen % 2 + 2 * (y_all % 2) + 4 * (z_all % 2)
    return (neighbour_table, parent_ids.reshape(-1).astype(jnp.int32), octant_ids.reshape(-1).astype(jnp.int32))


def draw_neighbours(key, part):
    return geometry(key)[0]


def draw_parent_index(key, part):
    return geometry(key)[1]


def draw_octant(key, part):
    return geometry(key)[2]


def draw_parent_dest(key, part):
    devices = N_SPACE
    parent_count = PARENT_DEV
    capacity = parent_count // 2
    slots_dev = parent_count + 2 * capacity
    first_key, second_key, third_key = jax.random.split(jax.random.fold_in(key, 29), 3)
    device_ids = jnp.arange(devices, dtype=jnp.int32)
    to_lower = jax.random.randint(first_key, (devices,), 0, capacity + 1, dtype=jnp.int32)
    to_upper = jax.random.randint(second_key, (devices,), 0, capacity + 1, dtype=jnp.int32)
    to_lower = jnp.where(device_ids == 0, 0, to_lower)
    to_upper = jnp.where(device_ids == devices - 1, 0, to_upper)
    centre = jax.random.randint(third_key, (), 1, devices - 1, dtype=jnp.int32)
    to_lower = jnp.where(device_ids == centre, 0, to_lower)
    to_upper = jnp.where(device_ids == centre, 0, to_upper)
    to_upper = jnp.where(device_ids == centre - 1, capacity, to_upper)
    to_lower = jnp.where(device_ids == centre + 1, capacity, to_lower)
    kept = parent_count - to_lower - to_upper
    zero_one = jnp.zeros((1,), jnp.int32)
    upper_prev = jnp.concatenate([zero_one, to_upper[:-1]])
    kept_prev = jnp.concatenate([zero_one, kept[:-1]])
    upper_prev_two = jnp.concatenate([zero_one, zero_one, to_upper[:-2]])
    order_ids = jnp.arange(parent_count, dtype=jnp.int32)[None, :]
    lower_count = to_lower[:, None]
    upper_count = to_upper[:, None]
    goes_lower = order_ids < lower_count
    goes_upper = order_ids >= parent_count - upper_count
    owner = jnp.where(goes_lower, device_ids[:, None] - 1, jnp.where(goes_upper, device_ids[:, None] + 1, device_ids[:, None]))
    slot = jnp.where(goes_lower, upper_prev_two[:, None] + kept_prev[:, None] + order_ids, jnp.where(goes_upper, order_ids - (parent_count - upper_count), upper_prev[:, None] + order_ids - lower_count))
    return (owner * slots_dev + slot).reshape(-1).astype(jnp.int32)


def steps_of(key, dims, cuts, least, largest):
    loudness, own = 1.0, jax.random.fold_in(key, 6)
    for dim, parts in cuts:
        draws = jnp.exp(jax.random.uniform(jax.random.fold_in(own, dim), (parts,), jnp.float32, least / len(cuts), largest / len(cuts)))
        loudness = loudness * jnp.repeat(draws, dims[dim] // parts).reshape([-1 if axis == dim else 1 for axis in range(len(dims))])
    return loudness


def normal_values(key, dims, spread, most, cuts=(), held_as=jnp.bfloat16):
    gain = steps_of(key, dims, cuts, -0.22, 0.18) if cuts else 1.0
    values = jax.random.normal(key, dims, jnp.float32) * spread * gain
    return jnp.minimum(jnp.maximum(values, -most), most).astype(held_as)


def setup_inputs(seed: int = 0) -> dict:
    key_of = jax.random.split(jax.random.key(seed), 10)
    return {
        "features": normal_values(key_of[0], (BRICKS, EDGE ** 3, FINE_CH), 1.0, 6.0, ((0, 8),)),
        "neighbours": draw_neighbours(jax.random.fold_in(key_of[9], 71), 0),
        "parent_index": draw_parent_index(jax.random.fold_in(key_of[9], 71), 0),
        "octant": draw_octant(jax.random.fold_in(key_of[9], 71), 0),
        "parent_dest": draw_parent_dest(jax.random.fold_in(key_of[9], 71), 0),
        "conv_fine": normal_values(key_of[5], (FINE_CH, 27 * FINE_CH), (27 * FINE_CH) ** -0.5, 0.109375, ((0, 4),)),
        "conv_down": normal_values(key_of[6], (COARSE_CH, 27 * FINE_CH), (27 * FINE_CH // 2) ** -0.5, 0.15625, ((0, 4),)),
        "conv_coarse": normal_values(key_of[7], (COARSE_CH, 27 * COARSE_CH), (27 * COARSE_CH // 4) ** -0.5, 0.15625, ((0, 4),)),
        "norm_gain": jnp.clip(1.0 + 0.15 * jax.random.normal(key_of[8], (COARSE_CH,), jnp.float32), 0.25, 1.75),
    }


offset_list = [(a, b, c) for a in (-1, 0, 1) for b in (-1, 0, 1) for c in (-1, 0, 1)]
around_list = [item for item in offset_list if item != (0, 0, 0)]
epsilon = 1e-06

def stride_span(first, number, stride):
    return slice(first, first + stride * (number - 1) + 1, stride)

def source_span(offset, length):
    if offset < 0:
        return slice(length - 1, length)
    if offset == 0:
        return slice(0, length)
    return slice(0, 1)

def target_span(offset, length):
    if offset < 0:
        return slice(0, 1)
    if offset == 0:
        return slice(1, length + 1)
    return slice(length + 1, length + 2)

def apply_taps(padded, weight, counts, stride):
    in_width = padded.shape[-1]
    accumulated = None
    for t, (a, b, c) in enumerate(offset_list):
        window = padded[:, stride_span(1 + a, counts[0], stride), stride_span(1 + b, counts[1], stride), stride_span(1 + c, counts[2], stride)]
        tap_block = weight[:, t * in_width:(t + 1) * in_width]
        product = lax.dot_general(window.reshape(-1, in_width), tap_block, (((1,), (1,)), ((), ())), preferred_element_type=jnp.float32)
        accumulated = product if accumulated is None else accumulated + product
    return accumulated.reshape((padded.shape[0],) + tuple(counts) + (weight.shape[0],))

def surround_all(pool_rows, brick_block, link_rows, lower_only):
    length = brick_block.shape[1]
    padded_size = length + 1 if lower_only else length + 2
    padded = jnp.zeros((brick_block.shape[0], padded_size, padded_size, padded_size, brick_block.shape[-1]), brick_block.dtype)
    padded = padded.at[:, 1:length + 1, 1:length + 1, 1:length + 1].set(brick_block)
    blank_index = pool_rows.shape[0] - 1
    for k, (a, b, c) in enumerate(around_list):
        if lower_only and max(a, b, c) > 0:
            continue
        row_index = jnp.where(link_rows[:, k] >= 0, link_rows[:, k], blank_index).astype(jnp.int32)
        fetched = jnp.take(pool_rows, row_index, axis=0)
        fetched = fetched[:, source_span(a, length), source_span(b, length), source_span(c, length)]
        padded = padded.at[:, target_span(a, length), target_span(b, length), target_span(c, length)].set(fetched)
    return padded

def assemble_slab(pieces, local_parent, octant):
    brick_count = pieces.shape[0]
    half_edge = pieces.shape[1]
    places = 2 * SLAB_Y * SLAB_Z
    x_bit = octant % 2
    y_pos = 2 * (local_parent // (SLAB_Z // 2)) + octant // 2 % 2
    z_pos = 2 * (local_parent % (SLAB_Z // 2)) + octant // 4
    position = x_bit + 2 * y_pos + 2 * SLAB_Y * z_pos
    matches = position[None, :] == jnp.arange(places, dtype=jnp.int32)[:, None]
    brick_ids = jnp.arange(brick_count, dtype=jnp.int32)
    row_index = jnp.where(jnp.any(matches, 1), lax.optimization_barrier(jnp.sum(jnp.where(matches, brick_ids[None, :], 0), 1)), brick_count).astype(jnp.int32)
    blank_row = jnp.zeros((1,) + pieces.shape[1:], pieces.dtype)
    placed = jnp.take(jnp.concatenate([pieces, blank_row], 0), row_index, axis=0)
    placed = placed.reshape(SLAB_Z, SLAB_Y, 2, half_edge, half_edge, half_edge, pieces.shape[-1])
    placed = placed.transpose(2, 3, 1, 4, 0, 5, 6)
    return placed.reshape(2 * half_edge, SLAB_Y * half_edge, SLAB_Z * half_edge, pieces.shape[-1])

def split_parents(coarse_slab):
    edge_cells = coarse_slab.shape[0]
    rows_y = coarse_slab.shape[1] // edge_cells
    rows_z = coarse_slab.shape[2] // edge_cells
    shaped = coarse_slab.reshape(edge_cells, rows_y, edge_cells, rows_z, edge_cells, coarse_slab.shape[-1])
    shaped = shaped.transpose(1, 3, 0, 2, 4, 5)
    return shaped.reshape(rows_y * rows_z, edge_cells ** 3, coarse_slab.shape[-1])

def reference(features, neighbours, parent_index, octant, parent_dest, conv_fine, conv_down, conv_coarse, norm_gain):
    half_edge = EDGE // 2
    brick_cubes = features.reshape(N_SPACE, BRICK_DEV, EDGE, EDGE, EDGE, FINE_CH)
    link_all = neighbours.reshape(N_SPACE, BRICK_DEV, 26)
    blank_row = jnp.zeros((1, EDGE, EDGE, EDGE, FINE_CH), features.dtype)
    feature_pool = jnp.concatenate([features.reshape(-1, EDGE, EDGE, EDGE, FINE_CH), blank_row], 0)

    def fine_step(inputs):
        padded = surround_all(feature_pool, inputs[0], inputs[1], False)
        return jnp.maximum(apply_taps(padded, conv_fine, (EDGE, EDGE, EDGE), 1), 0.0).astype(jnp.bfloat16)
    hidden = lax.map(fine_step, (brick_cubes, link_all))
    hidden_pool = jnp.concatenate([hidden.reshape(-1, EDGE, EDGE, EDGE, FINE_CH), blank_row.astype(hidden.dtype)], 0)

    def down_step(inputs):
        padded = surround_all(hidden_pool, inputs[0], inputs[1], True)
        return jnp.maximum(apply_taps(padded, conv_down, (half_edge, half_edge, half_edge), 2), 0.0).astype(jnp.bfloat16)
    pieces = lax.map(down_step, (hidden, link_all))
    device_ids = jnp.arange(N_SPACE, dtype=jnp.int32)
    local_parent = parent_index.reshape(N_SPACE, BRICK_DEV) - PARENT_DEV * device_ids[:, None]
    octants = octant.reshape(N_SPACE, BRICK_DEV)
    slabs = lax.map(lambda inputs: assemble_slab(inputs[0], inputs[1], inputs[2]), (pieces, local_parent, octants))
    span_y = slabs.shape[2]
    span_z = slabs.shape[3]
    grid_all = jnp.pad(slabs.reshape(N_SPACE * EDGE, span_y, span_z, COARSE_CH), ((1, 1), (1, 1), (1, 1), (0, 0)))

    def coarse_step(device):
        window = lax.dynamic_slice_in_dim(grid_all, (device * EDGE).astype(jnp.int32), EDGE + 2, 0)
        convolved = apply_taps(window[None], conv_coarse, (EDGE, span_y, span_z), 1)[0].astype(jnp.bfloat16)
        return split_parents(convolved)
    parents = lax.map(coarse_step, device_ids).reshape(N_SPACE * PARENT_DEV, EDGE ** 3, COARSE_CH)
    values = parents.astype(jnp.float32)
    cell_power = lax.optimization_barrier(jnp.sum(values * values, -1))
    normed = (values * lax.rsqrt(cell_power[..., None] / COARSE_CH + epsilon) * norm_gain).astype(jnp.bfloat16)
    result = jnp.zeros((N_SPACE * SLOTS_DEV, EDGE ** 3, COARSE_CH), jnp.bfloat16)
    result = result.at[parent_dest].set(normed)
    return result.transpose(2, 0, 1).reshape(COARSE_CH, N_SPACE * SLOTS_DEV * EDGE ** 3)
```

```python
import functools

import jax
import jax.numpy as jnp
import numpy as np
from jax import lax
from jax.experimental import pallas as pl
from jax.experimental.pallas import tpu as pltpu
from jax.sharding import PartitionSpec as P

EDGE = 4
SLAB_Y = 4
SLAB_Z = 4
PAD = EDGE + 2
LOW = EDGE + 1
HALF = EDGE // 2
FACE = EDGE * EDGE
CY = SLAB_Y * HALF
CZ = SLAB_Z * HALF
CLAYER = CY * CZ
CX = 2 * HALF
TAPS2 = 9
epsilon = 1e-06
FAR = 1 << 20
BF = jnp.bfloat16
F32 = jnp.float32
NT = (((1,), (1,)), ((), ()))


def iota(shape, dim):
    return lax.broadcasted_iota(jnp.int32, shape, dim)


def one(cond):
    return jnp.where(cond, 1.0, 0.0).astype(BF)


def pick(a, b):
    return jnp.dot(a, b, preferred_element_type=F32)


def tap2(b, c):
    return 3 * (b + 1) + c + 1


def source(pos):
    if pos == 0:
        return -1, EDGE - 1
    if pos == EDGE + 1:
        return 1, 0
    return 0, pos - 1


def table(n_chan, fine):
    wide = fine // n_chan
    r = np.arange(n_chan * EDGE * wide)[:, None]
    q = np.arange(n_chan * EDGE * wide)[None, :]
    group = EDGE * wide
    perm = (r % group) // wide * fine + r // group * wide + r % wide == q
    return jnp.asarray(np.asarray(perm, np.float32).astype(jnp.bfloat16))


def fused_kernel(
    n_space, n_chan, bricks, slots,
    feat_hbm, nbr_hbm, parent_hbm, octant_hbm, dest_hbm, wf_hbm, wd_hbm, wc_hbm, gain_hbm, perm_hbm,
    out,
    feat, nbr, wf, wt, gain, parent_in, octant_in, dest_in, meta, wd, wc, perm,
    fh, mh, pbuf, g_buf, qbuf, c_buf, cp, cn, e_buf, hot_e, hot_o, pb, pw, ohd,
    wsem, s1, r1, s2, r2, hs2, hr2, s3, r3, hs3, hr3, s4, r4, ws4, wr4,
):
    sp = lax.axis_index("space")
    me = lax.axis_index("chan")
    has_prev = sp > 0
    has_next = sp < n_space - 1
    fine = feat.shape[2]
    wide = fine // n_chan
    parents = dest_in.shape[1]
    cells = EDGE**3
    own_d = wd.shape[0]
    coarse = own_d * n_chan
    group = EDGE * wide
    line = EDGE * bricks
    side = HALF * bricks

    def rc(src, dst, ss, rs, space, chan):
        return pltpu.make_async_remote_copy(
            src_ref=src,
            dst_ref=dst,
            send_sem=ss,
            recv_sem=rs,
            device_id={"space": space, "chan": chan},
            device_id_type=pl.DeviceIdType.MESH,
        )

    peers = [lax.rem(me + k, n_chan) for k in range(1, n_chan)]
    barrier = pltpu.get_barrier_semaphore()

    def greet(space, chan):
        pl.semaphore_signal(
            barrier,
            inc=1,
            device_id={"space": space, "chan": chan},
            device_id_type=pl.DeviceIdType.MESH,
        )

    @pl.when(has_prev)
    def _():
        for chan in range(n_chan):
            greet(sp - 1, chan)

    @pl.when(has_next)
    def _():
        for chan in range(n_chan):
            greet(sp + 1, chan)

    for chan in peers:
        greet(sp, chan)

    loads = [
        pltpu.make_async_copy(src, dst, wsem.at[k])
        for k, (src, dst) in enumerate(
            (
                (nbr_hbm, nbr),
                (feat_hbm, feat),
                (parent_hbm, parent_in),
                (octant_hbm, octant_in),
                (dest_hbm, dest_in),
                (wf_hbm, wf),
                (perm_hbm, perm),
                (wd_hbm, wd),
                (gain_hbm, gain),
                (wc_hbm, wc),
            )
        )
    ]
    for load in loads:
        load.start()

    @pl.when(jnp.logical_not(has_prev))
    def _():
        fh[0] = jnp.zeros(fh.shape[1:], BF)
        mh[0] = jnp.zeros(mh.shape[1:], jnp.int32)
        for s in range(n_chan):
            g_buf[s, 0] = jnp.zeros(g_buf.shape[2:], BF)
        cp[...] = jnp.zeros(cp.shape, BF)
        pb[0] = jnp.zeros(pb.shape[1:], BF)
        pw[0] = jnp.zeros(pw.shape[1:], F32)

    @pl.when(jnp.logical_not(has_next))
    def _():
        fh[1] = jnp.zeros(fh.shape[1:], BF)
        mh[1] = jnp.zeros(mh.shape[1:], jnp.int32)
        cn[...] = jnp.zeros(cn.shape, BF)
        pb[2] = jnp.zeros(pb.shape[1:], BF)
        pw[2] = jnp.zeros(pw.shape[1:], F32)

    reach = PAD * fine
    for z in range(EDGE):
        for bc in range(TAPS2):
            at = bc * reach
            rows = slice(z * wide, (z + 1) * wide)
            if z > 0:
                wt[rows, at : at + z * fine] = jnp.zeros((wide, z * fine), BF)
            if z < EDGE - 1:
                wt[rows, at + (z + 3) * fine : at + reach] = jnp.zeros((wide, (EDGE - 1 - z) * fine), BF)
    meta[...] = jnp.zeros(meta.shape, jnp.int32)

    for load in loads[2:5]:
        load.wait()
    local = parent_in[...] - sp * parents
    octant = octant_in[...]
    y_pos = 2 * (local // (SLAB_Z // 2)) + octant // 2 % 2
    z_pos = 2 * (local % (SLAB_Z // 2)) + octant // 4
    meta[0:1, 0:bricks] = octant % 2 + 2 * y_pos + 2 * SLAB_Y * z_pos
    meta[1:2, 0:parents] = dest_in[...] - (sp - 1) * slots

    up_feat = rc(feat_hbm.at[:, pl.ds((EDGE - 1) * FACE, FACE), :], fh.at[0], s1.at[0, 0], r1.at[0, 0], sp + 1, me)
    up_meta = rc(meta, mh.at[0], s1.at[0, 1], r1.at[0, 1], sp + 1, me)
    dn_feat = rc(feat_hbm.at[:, pl.ds(0, FACE), :], fh.at[1], s1.at[1, 0], r1.at[1, 0], sp - 1, me)
    dn_meta = rc(meta, mh.at[1], s1.at[1, 1], r1.at[1, 1], sp - 1, me)

    pl.semaphore_wait(
        barrier, n_chan - 1 + n_chan * (has_prev.astype(jnp.int32) + has_next.astype(jnp.int32))
    )

    @pl.when(has_next)
    def _():
        up_feat.start()
        up_meta.start()

    @pl.when(has_prev)
    def _():
        dn_feat.start()
        dn_meta.start()

    for load in loads[0:2]:
        load.wait()
    raw = nbr[...]
    loc = jnp.where(raw >= 0, raw - bricks * (sp - 1), -FAR)
    here = iota((bricks, 1), 0) + bricks

    def loc_of(a, b, c):
        k = 9 * (a + 1) + tap2(b, c)
        if k == 13:
            return here
        k = k - (k > 13)
        return loc[:, k : k + 1]

    def place(a, first, sources, planes):
        wide_k = sources.shape[0]
        col = iota((bricks, wide_k), 1)
        keys = {
            (b, c): jnp.broadcast_to((loc_of(a, b, c) - first) * FACE, (bricks, wide_k))
            for b in (-1, 0, 1)
            for c in (-1, 0, 1)
        }
        for zq in range(PAD):
            c, sz = source(zq)
            hots = []
            for yq in range(PAD):
                b, sy = source(yq)
                hots.append(one(col == keys[b, c] + (sy * EDGE + sz)))
            placed = pick(jnp.concatenate(hots, axis=0), sources).astype(BF)
            for i, xq in enumerate(planes):
                pbuf[xq, :, :, zq * fine : (zq + 1) * fine] = placed[:, i * fine : (i + 1) * fine].reshape(
                    PAD, bricks, fine
                )

    def plane(i):
        return feat[:, i * FACE : (i + 1) * FACE, :].reshape(bricks * FACE, fine)

    place(0, bricks, jnp.concatenate([plane(i) for i in range(EDGE)], axis=1), range(1, EDGE + 1))

    loads[5].wait()
    for z in range(EDGE):
        for bc in range(TAPS2):
            at = bc * reach + z * fine
            wt[z * wide : (z + 1) * wide, at : at + 3 * fine] = wf[:, bc * 3 * fine : (bc + 1) * 3 * fine]

    def hidden(planes):
        parts = []
        for a in range(3):
            for b in range(3):
                parts.append(
                    jnp.concatenate([pbuf[x + a, b : b + EDGE].reshape(line, reach) for x in planes], axis=0)
                )
        total = lax.dot_general(jnp.concatenate(parts, axis=1), wt[...], NT, preferred_element_type=F32)
        total = jnp.maximum(total, 0.0).astype(BF)
        for i, x in enumerate(planes):
            g_buf[me, x + 1] = total[i * line : (i + 1) * line]

    spans = ((2, EDGE - 2), (EDGE, 1), (1, 1))

    def hid_copy(j, k, chan):
        ref = g_buf.at[me, pl.ds(*spans[j])]
        return rc(ref, ref, s2.at[j, k], r2.at[j, me], sp, chan)

    def hid_wait(j):
        for k in range(1, n_chan):
            src = lax.rem(me + k, n_chan)
            ref = g_buf.at[src, pl.ds(*spans[j])]
            rc(ref, ref, s2.at[j, 0], r2.at[j, src], sp, src).wait_recv()

    hidden(list(range(1, EDGE - 1)))
    for k, chan in enumerate(peers):
        hid_copy(0, k, chan).start()

    @pl.when(has_next)
    def _():
        dn_feat.wait_recv()
        dn_meta.wait_recv()

    place(1, bricks, jnp.concatenate([plane(0), fh[1].reshape(bricks * FACE, fine)], axis=0), [EDGE + 1])

    @pl.when(has_prev)
    def _():
        up_feat.wait_recv()
        up_meta.wait_recv()

    place(-1, 0, jnp.concatenate([fh[0].reshape(bricks * FACE, fine), plane(EDGE - 1)], axis=0), [0])
    hidden([0, EDGE - 1])

    @pl.when(has_next)
    def _():
        for chan in range(n_chan):
            rc(g_buf.at[me, EDGE], g_buf.at[me, 0], hs2.at[chan], hr2.at[me], sp + 1, chan).start()

    for j in (1, 2):
        for k, chan in enumerate(peers):
            hid_copy(j, k, chan).start()

    lanes = meta.shape[1]
    lane_par = jnp.where(
        iota((lanes, parents * cells), 1) // cells == iota((lanes, parents * cells), 0), 1.0, 0.0
    )

    def dest_table(k):
        block = meta[...] if k == 1 else mh[k // 2]
        rel = jnp.dot(block.astype(F32), lane_par, preferred_element_type=F32)[1:2].astype(jnp.int32)
        slot = rel - (2 - k) * slots
        target = slot * cells + iota((1, parents * cells), 1) % cells
        ids = iota((slots * cells, parents * cells), 0)
        ohd[k] = one(ids == jnp.where((slot >= 0) & (slot < slots), target, -1))

    n_own = HALF**3 * bricks
    spread = jnp.where(iota((lanes, n_own), 1) % bricks == iota((lanes, n_own), 0), 1.0, 0.0)

    def codes(block, n):
        code = jnp.dot(block.astype(F32), spread[:, 0:n], preferred_element_type=F32)[0:1].astype(jnp.int32)
        return code % 2, code // 2 % SLAB_Y, code // (2 * SLAB_Y)

    def wants(n, bc):
        at = iota((CLAYER, n), 0)
        par, yz = at // FACE, at % FACE
        y = par // (SLAB_Z // 2) * EDGE + yz // EDGE + bc // 3 - 1
        z = par % (SLAB_Z // 2) * EDGE + yz % EDGE + bc % 3 - 1
        return jnp.where((y >= 0) & (y < CY) & (z >= 0) & (z < CZ), y * CZ + z, FAR)

    x_bit, y_at, z_at = codes(meta[...], n_own)
    sub = iota((1, n_own), 1) // bricks
    key = (2 * y_at + sub % HALF) * CZ + 2 * z_at + sub // (HALF * HALF)
    layer = 2 * x_bit + sub // HALF % HALF
    for bc in range(TAPS2):
        want = wants(n_own, bc)
        for x in range(CX):
            hot_e[x, bc * CLAYER : (bc + 1) * CLAYER] = one(want == jnp.where(layer == x, key, -1))

    n_out = HALF * HALF * bricks
    for k in range(2):
        x_bit, y_at, z_at = codes(mh[k], n_out)
        sub = iota((1, n_out), 1) // bricks
        key = (2 * y_at + sub % HALF) * CZ + 2 * z_at + sub // HALF
        key = jnp.where(x_bit == 1 - k, key, -1)
        for bc in range(TAPS2):
            hot_o[k, bc * CLAYER : (bc + 1) * CLAYER] = one(wants(n_out, bc) == key)

    for k in range(3):
        dest_table(k)

    for load in loads[6:8]:
        load.wait()

    for j in range(3):
        hid_wait(j)

    def unpack(first, number):
        joined = jnp.concatenate(
            [g_buf[s, first : first + number].reshape(number * line, group) for s in range(n_chan)], axis=1
        )
        return pick(joined, perm[...]).astype(BF)

    full = EDGE * fine
    moved = unpack(1, EDGE)
    for x in range(EDGE):
        qbuf[x + 1, 1:LOW, :, fine : LOW * fine] = moved[x * line : (x + 1) * line].reshape(EDGE, bricks, full)

    def hot_rows(a, c, n):
        col = iota((bricks, n), 1)
        rows = []
        for yq in range(LOW):
            b, sy = source(yq)
            where = loc_of(a, b, c)
            where = jnp.where(where >= bricks, where - bricks, where + line) + sy * bricks
            rows.append(one(col == where))
        return jnp.concatenate(rows, axis=0)

    tail = fine * (EDGE - 1)
    edge_y = pick(
        one(iota((bricks, bricks), 1) == loc_of(0, -1, 0) - bricks),
        jnp.concatenate([moved[x * line + line - bricks : (x + 1) * line] for x in range(EDGE)], axis=1),
    ).astype(BF)
    edge_z = pick(
        hot_rows(0, -1, line), jnp.concatenate([moved[x * line : (x + 1) * line, tail:] for x in range(EDGE)], axis=1)
    ).astype(BF)
    for x in range(EDGE):
        qbuf[x + 1, 0, :, fine : LOW * fine] = edge_y[:, x * full : (x + 1) * full]
        qbuf[x + 1, :, :, 0:fine] = edge_z[:, x * fine : (x + 1) * fine].reshape(LOW, bricks, fine)

    @pl.when(has_prev)
    def _():
        for chan in range(n_chan):
            rc(g_buf.at[chan, 0], g_buf.at[chan, 0], hs2.at[chan], hr2.at[chan], sp - 1, chan).wait_recv()

    joint = jnp.concatenate([moved[tail // fine * line :], unpack(0, 1)], axis=0)
    qbuf[0, :, :, fine : LOW * fine] = pick(hot_rows(-1, 0, 2 * line), joint).astype(BF).reshape(LOW, bricks, full)
    qbuf[0, :, :, 0:fine] = pick(hot_rows(-1, -1, 2 * line), joint[:, tail:]).astype(BF).reshape(LOW, bricks, fine)

    stacked = []
    for qz in range(HALF):
        for qx in range(HALF):
            for qy in range(HALF):
                stacked.append(
                    jnp.concatenate(
                        [
                            qbuf[2 * qx + a, 2 * qy + b, :, 2 * qz * fine : (2 * qz + 3) * fine]
                            for a in range(3)
                            for b in range(3)
                        ],
                        axis=1,
                    )
                )
    pieces = lax.dot_general(jnp.concatenate(stacked, axis=0), wd[...], NT, preferred_element_type=F32)
    pieces = jnp.maximum(pieces, 0.0)
    part = 2 * side
    c_buf[me] = jnp.concatenate([pieces[h * part : (h + 1) * part] for h in range(HALF)], axis=1).astype(BF)

    for k, chan in enumerate(peers):
        rc(c_buf.at[me], c_buf.at[me], s3.at[k], r3.at[me], sp, chan).start()

    @pl.when(has_next)
    def _():
        for chan in range(n_chan):
            rc(c_buf.at[me, pl.ds(side, side)], cp.at[me], hs3.at[0, chan], hr3.at[0, me], sp + 1, chan).start()

    @pl.when(has_prev)
    def _():
        for chan in range(n_chan):
            rc(c_buf.at[me, pl.ds(0, side)], cn.at[me], hs3.at[1, chan], hr3.at[1, me], sp - 1, chan).start()

    for load in loads[8:]:
        load.wait()
    own = gain.shape[1]
    gain_col = jnp.sum(
        jnp.where(iota((own, own), 0) == iota((own, own), 1), gain[...], 0.0), axis=1, keepdims=True
    )

    for k in range(1, n_chan):
        src = lax.rem(me + k, n_chan)
        rc(c_buf.at[src], c_buf.at[src], s3.at[0], r3.at[src], sp, src).wait_recv()

    def all_channels(buf):
        return jnp.concatenate(
            [
                jnp.concatenate([buf[s][:, h * own_d : (h + 1) * own_d] for s in range(n_chan)], axis=1)
                for h in range(HALF)
            ],
            axis=0,
        )

    def coarse_taps(a, total):
        for bc in range(TAPS2):
            block = jnp.concatenate(
                [
                    e_buf[x + a, bc * CLAYER + g * FACE : bc * CLAYER + (g + 1) * FACE, :]
                    for g in range(parents)
                    for x in range(CX)
                ],
                axis=0,
            )
            t = a * TAPS2 + bc
            term = lax.dot_general(wc[:, t * coarse : (t + 1) * coarse], block, NT, preferred_element_type=F32)
            total = term if total is None else total + term
        return total

    inside = all_channels(c_buf)
    for x in range(CX):
        e_buf[x + 1] = pick(hot_e[x], inside).astype(BF)
    total = coarse_taps(1, None)

    @pl.when(has_prev)
    def _():
        for chan in range(n_chan):
            rc(cp.at[chan], cp.at[chan], hs3.at[0, chan], hr3.at[0, chan], sp - 1, chan).wait_recv()

    @pl.when(has_next)
    def _():
        for chan in range(n_chan):
            rc(cn.at[chan], cn.at[chan], hs3.at[1, chan], hr3.at[1, chan], sp + 1, chan).wait_recv()

    e_buf[0] = pick(hot_o[0], all_channels(cp)).astype(BF)
    e_buf[CX + 1] = pick(hot_o[1], all_channels(cn)).astype(BF)
    total = coarse_taps(0, total)
    total = coarse_taps(2, total)
    rounded = total.astype(BF)
    pb[1] = rounded
    values = rounded.astype(F32)
    pw[1, me] = jnp.sum(values * values, axis=0, keepdims=True)

    for k, chan in enumerate(peers):
        rc(pw.at[1, me], pw.at[1, me], ws4.at[1, k], wr4.at[1, me], sp, chan).start()

    @pl.when(has_next)
    def _():
        rc(pb.at[1], pb.at[0], s4.at[0], r4.at[0], sp + 1, me).start()
        for chan in range(n_chan):
            rc(pw.at[1, me], pw.at[0, me], ws4.at[0, chan], wr4.at[0, me], sp + 1, chan).start()

    @pl.when(has_prev)
    def _():
        rc(pb.at[1], pb.at[2], s4.at[1], r4.at[1], sp - 1, me).start()
        for chan in range(n_chan):
            rc(pw.at[1, me], pw.at[2, me], ws4.at[2, chan], wr4.at[2, me], sp - 1, chan).start()

    def normed(k):
        power = pw[k, 0]
        for s in range(1, n_chan):
            power = power + pw[k, s]
        scaled = pb[k].astype(F32) * lax.rsqrt(power / coarse + epsilon) * gain_col
        return lax.dot_general(scaled.astype(BF), ohd[k], NT, preferred_element_type=F32)

    for k in range(1, n_chan):
        src = lax.rem(me + k, n_chan)
        rc(pw.at[1, src], pw.at[1, src], ws4.at[1, 0], wr4.at[1, src], sp, src).wait_recv()
    result = normed(1)

    @pl.when(has_prev)
    def _():
        rc(pb.at[0], pb.at[0], s4.at[0], r4.at[0], sp - 1, me).wait_recv()
        for chan in range(n_chan):
            rc(pw.at[0, chan], pw.at[0, chan], ws4.at[0, chan], wr4.at[0, chan], sp - 1, chan).wait_recv()

    @pl.when(has_next)
    def _():
        rc(pb.at[2], pb.at[2], s4.at[1], r4.at[1], sp + 1, me).wait_recv()
        for chan in range(n_chan):
            rc(pw.at[2, chan], pw.at[2, chan], ws4.at[2, chan], wr4.at[2, chan], sp + 1, chan).wait_recv()

    out[...] = (result + normed(0) + normed(2)).astype(BF)

    for k, chan in enumerate(peers):
        for j in range(3):
            hid_copy(j, k, chan).wait_send()
        rc(c_buf.at[me], c_buf.at[me], s3.at[k], r3.at[me], sp, chan).wait_send()
        rc(pw.at[1, me], pw.at[1, me], ws4.at[1, k], wr4.at[1, me], sp, chan).wait_send()

    @pl.when(has_next)
    def _():
        up_meta.wait_send()
        up_feat.wait_send()
        rc(pb.at[1], pb.at[0], s4.at[0], r4.at[0], sp + 1, me).wait_send()
        for chan in range(n_chan):
            rc(g_buf.at[me, EDGE], g_buf.at[me, 0], hs2.at[chan], hr2.at[me], sp + 1, chan).wait_send()
            rc(c_buf.at[me, pl.ds(side, side)], cp.at[me], hs3.at[0, chan], hr3.at[0, me], sp + 1, chan).wait_send()
            rc(pw.at[1, me], pw.at[0, me], ws4.at[0, chan], wr4.at[0, me], sp + 1, chan).wait_send()

    @pl.when(has_prev)
    def _():
        dn_meta.wait_send()
        dn_feat.wait_send()
        rc(pb.at[1], pb.at[2], s4.at[1], r4.at[1], sp - 1, me).wait_send()
        for chan in range(n_chan):
            rc(c_buf.at[me, pl.ds(0, side)], cn.at[me], hs3.at[1, chan], hr3.at[1, me], sp - 1, chan).wait_send()
            rc(pw.at[1, me], pw.at[2, me], ws4.at[2, chan], wr4.at[2, me], sp - 1, chan).wait_send()


def body(n_space, n_chan, features, neighbours, parent_index, octant, parent_dest, conv_fine, conv_down, conv_coarse, norm_gain):
    bricks, _, fine = features.shape
    parents = parent_dest.shape[0]
    slots = 2 * parents
    own_d = conv_down.shape[0]
    own = conv_coarse.shape[0]
    cells = EDGE**3
    coarse = own_d * n_chan
    group = EDGE * fine // n_chan
    vmem = pl.BlockSpec(memory_space=pltpu.VMEM)
    hbm = pl.BlockSpec(memory_space=pltpu.HBM)
    dma = pltpu.SemaphoreType.DMA
    return pl.pallas_call(
        functools.partial(fused_kernel, n_space, n_chan, bricks, slots),
        out_shape=jax.ShapeDtypeStruct((own, slots * cells), BF),
        in_specs=[hbm] * 10,
        out_specs=vmem,
        scratch_shapes=[
            pltpu.VMEM(features.shape, BF),
            pltpu.VMEM(neighbours.shape, jnp.int32),
            pltpu.VMEM(conv_fine.shape, BF),
            pltpu.VMEM((group, TAPS2 * PAD * fine), BF),
            pltpu.VMEM((1, own), F32),
            pltpu.VMEM((1, bricks), jnp.int32),
            pltpu.VMEM((1, bricks), jnp.int32),
            pltpu.VMEM((1, parents), jnp.int32),
            pltpu.VMEM((8, 128), jnp.int32),
            pltpu.VMEM(conv_down.shape, BF),
            pltpu.VMEM(conv_coarse.shape, BF),
            pltpu.VMEM((n_chan * group, n_chan * group), BF),
            pltpu.VMEM((2, bricks, FACE, fine), BF),
            pltpu.VMEM((2, 8, 128), jnp.int32),
            pltpu.VMEM((PAD, PAD, bricks, PAD * fine), BF),
            pltpu.VMEM((n_chan, LOW, EDGE * bricks, group), BF),
            pltpu.VMEM((LOW, LOW, bricks, LOW * fine), BF),
            pltpu.VMEM((n_chan, HALF * HALF * bricks, HALF * own_d), BF),
            pltpu.VMEM((n_chan, HALF * bricks, HALF * own_d), BF),
            pltpu.VMEM((n_chan, HALF * bricks, HALF * own_d), BF),
            pltpu.VMEM((CX + 2, TAPS2 * CLAYER, coarse), BF),
            pltpu.VMEM((CX, TAPS2 * CLAYER, HALF**3 * bricks), BF),
            pltpu.VMEM((2, TAPS2 * CLAYER, HALF**2 * bricks), BF),
            pltpu.VMEM((3, own, parents * cells), BF),
            pltpu.VMEM((3, n_chan, 1, parents * cells), F32),
            pltpu.VMEM((3, slots * cells, parents * cells), BF),
            dma((10,)),
            dma((2, 2)),
            dma((2, 2)),
            dma((3, n_chan - 1)),
            dma((3, n_chan)),
            dma((n_chan,)),
            dma((n_chan,)),
            dma((n_chan - 1,)),
            dma((n_chan,)),
            dma((2, n_chan)),
            dma((2, n_chan)),
            dma((2,)),
            dma((2,)),
            dma((3, n_chan)),
            dma((3, n_chan)),
        ],
        compiler_params=pltpu.CompilerParams(
            collective_id=0, has_side_effects=True, vmem_limit_bytes=66900000
        ),
    )(
        features,
        neighbours,
        parent_index.reshape(1, -1),
        octant.reshape(1, -1),
        parent_dest.reshape(1, -1),
        conv_fine,
        conv_down,
        conv_coarse,
        norm_gain.reshape(1, -1),
        table(n_chan, fine),
    )


def solution(mesh):
    sizes = dict(mesh.shape)
    return jax.shard_map(
        functools.partial(body, sizes["space"], sizes["chan"]),
        mesh=mesh,
        in_specs=(
            P("space", None, None),
            P("space", None),
            P("space"),
            P("space"),
            P("space"),
            P("chan", None),
            P("chan", None),
            P("chan", None),
            P("chan"),
        ),
        out_specs=P("chan", "space"),
        check_vma=False,
    )
```

```python
import functools

import jax
import jax.numpy as jnp
import numpy as np
from jax import lax
from jax.experimental import pallas as pl
from jax.experimental.pallas import tpu as pltpu
from jax.sharding import PartitionSpec as P

EDGE = 4
SLAB_Y = 4
SLAB_Z = 4
PAD = EDGE + 2
LOW = EDGE + 1
HALF = EDGE // 2
FACE = EDGE * EDGE
CY = SLAB_Y * HALF
CZ = SLAB_Z * HALF
CLAYER = CY * CZ
CX = 2 * HALF
TAPS2 = 9
epsilon = 1e-06
FAR = 1 << 20
BF = jnp.bfloat16
F32 = jnp.float32
NT = (((1,), (1,)), ((), ()))


def iota(shape, dim):
    return lax.broadcasted_iota(jnp.int32, shape, dim)


def one(cond):
    return jnp.where(cond, 1.0, 0.0).astype(BF)


def pick(a, b):
    return jnp.dot(a, b, preferred_element_type=F32)


def tap2(b, c):
    return 3 * (b + 1) + c + 1


def source(pos):
    if pos == 0:
        return -1, EDGE - 1
    if pos == EDGE + 1:
        return 1, 0
    return 0, pos - 1


def table(n_chan, fine):
    wide = fine // n_chan
    r = np.arange(n_chan * EDGE * wide)[:, None]
    q = np.arange(n_chan * EDGE * wide)[None, :]
    group = EDGE * wide
    perm = (r % group) // wide * fine + r // group * wide + r % wide == q
    return jnp.asarray(np.asarray(perm, np.float32).astype(jnp.bfloat16))


def fused_kernel(
    n_space, n_chan, bricks, slots,
    feat_hbm, nbr_hbm, parent_hbm, octant_hbm, dest_hbm, wf_hbm, wd_hbm, wc_hbm, gain_hbm, perm_hbm,
    out,
    feat, nbr, wf, wt, gain, parent_in, octant_in, dest_in, meta, wd, wc, perm,
    fh, mh, pbuf, part_h, g_buf, qbuf, c_buf, cp, cn, e_buf, hot_e, hot_o, pb, pw, ohd,
    wsem, s1, r1, s2, r2, hs2, hr2, s3, r3, hs3, hr3, s4, r4, ws4, wr4,
):
    sp = lax.axis_index("space")
    me = lax.axis_index("chan")
    has_prev = sp > 0
    has_next = sp < n_space - 1
    fine = feat.shape[2]
    wide = fine // n_chan
    parents = dest_in.shape[1]
    cells = EDGE**3
    own_d = wd.shape[0]
    coarse = own_d * n_chan
    group = EDGE * wide
    line = EDGE * bricks
    side = HALF * bricks

    def rc(src, dst, ss, rs, space, chan):
        return pltpu.make_async_remote_copy(
            src_ref=src,
            dst_ref=dst,
            send_sem=ss,
            recv_sem=rs,
            device_id={"space": space, "chan": chan},
            device_id_type=pl.DeviceIdType.MESH,
        )

    peers = [lax.rem(me + k, n_chan) for k in range(1, n_chan)]
    barrier = pltpu.get_barrier_semaphore()

    def greet(space, chan):
        pl.semaphore_signal(
            barrier,
            inc=1,
            device_id={"space": space, "chan": chan},
            device_id_type=pl.DeviceIdType.MESH,
        )

    @pl.when(has_prev)
    def _():
        greet(sp - 1, me)

    @pl.when(has_next)
    def _():
        greet(sp + 1, me)

    for chan in peers:
        greet(sp, chan)

    loads = [
        pltpu.make_async_copy(src, dst, wsem.at[k])
        for k, (src, dst) in enumerate(
            (
                (nbr_hbm, nbr),
                (feat_hbm, feat),
                (parent_hbm, parent_in),
                (octant_hbm, octant_in),
                (dest_hbm, dest_in),
                (wf_hbm, wf),
                (perm_hbm, perm),
                (wd_hbm, wd),
                (gain_hbm, gain),
                (wc_hbm, wc),
            )
        )
    ]
    for load in loads:
        load.start()

    up_feat = rc(feat_hbm.at[:, pl.ds((EDGE - 1) * FACE, FACE), :], fh.at[0], s1.at[0, 0], r1.at[0, 0], sp + 1, me)
    up_meta = rc(meta, mh.at[0], s1.at[0, 1], r1.at[0, 1], sp + 1, me)
    dn_feat = rc(feat_hbm.at[:, pl.ds(0, FACE), :], fh.at[1], s1.at[1, 0], r1.at[1, 0], sp - 1, me)
    dn_meta = rc(meta, mh.at[1], s1.at[1, 1], r1.at[1, 1], sp - 1, me)

    pl.semaphore_wait(barrier, n_chan - 1 + has_prev.astype(jnp.int32) + has_next.astype(jnp.int32))

    @pl.when(has_next)
    def _():
        up_feat.start()

    @pl.when(has_prev)
    def _():
        dn_feat.start()

    @pl.when(jnp.logical_not(has_prev))
    def _():
        fh[0] = jnp.zeros(fh.shape[1:], BF)
        mh[0] = jnp.zeros(mh.shape[1:], jnp.int32)
        for s in range(n_chan):
            g_buf[s, 0] = jnp.zeros(g_buf.shape[2:], BF)
        cp[...] = jnp.zeros(cp.shape, BF)
        pb[0] = jnp.zeros(pb.shape[1:], BF)
        pw[0] = jnp.zeros(pw.shape[1:], F32)

    @pl.when(jnp.logical_not(has_next))
    def _():
        fh[1] = jnp.zeros(fh.shape[1:], BF)
        mh[1] = jnp.zeros(mh.shape[1:], jnp.int32)
        cn[...] = jnp.zeros(cn.shape, BF)
        pb[2] = jnp.zeros(pb.shape[1:], BF)
        pw[2] = jnp.zeros(pw.shape[1:], F32)

    reach = PAD * fine
    for z in range(EDGE):
        for bc in range(TAPS2):
            at = bc * reach
            rows = slice(z * wide, (z + 1) * wide)
            if z > 0:
                wt[rows, at : at + z * fine] = jnp.zeros((wide, z * fine), BF)
            if z < EDGE - 1:
                wt[rows, at + (z + 3) * fine : at + reach] = jnp.zeros((wide, (EDGE - 1 - z) * fine), BF)
    meta[...] = jnp.zeros(meta.shape, jnp.int32)

    for load in loads[2:5]:
        load.wait()
    local = parent_in[...] - sp * parents
    octant = octant_in[...]
    y_pos = 2 * (local // (SLAB_Z // 2)) + octant // 2 % 2
    z_pos = 2 * (local % (SLAB_Z // 2)) + octant // 4
    meta[0:1, 0:bricks] = octant % 2 + 2 * y_pos + 2 * SLAB_Y * z_pos
    meta[1:2, 0:parents] = dest_in[...] - (sp - 1) * slots

    @pl.when(has_next)
    def _():
        up_meta.start()

    @pl.when(has_prev)
    def _():
        dn_meta.start()

    for load in loads[0:2]:
        load.wait()
    raw = nbr[...]
    loc = jnp.where(raw >= 0, raw - bricks * (sp - 1), -FAR)
    here = iota((bricks, 1), 0) + bricks

    def loc_of(a, b, c):
        k = 9 * (a + 1) + tap2(b, c)
        if k == 13:
            return here
        k = k - (k > 13)
        return loc[:, k : k + 1]

    def place(a, first, sources, planes):
        wide_k = sources.shape[0]
        col = iota((bricks, wide_k), 1)
        keys = {
            (b, c): jnp.broadcast_to((loc_of(a, b, c) - first) * FACE, (bricks, wide_k))
            for b in (-1, 0, 1)
            for c in (-1, 0, 1)
        }
        for zq in range(PAD):
            c, sz = source(zq)
            hots = []
            for yq in range(PAD):
                b, sy = source(yq)
                hots.append(one(col == keys[b, c] + (sy * EDGE + sz)))
            placed = pick(jnp.concatenate(hots, axis=0), sources).astype(BF)
            for i, xq in enumerate(planes):
                pbuf[xq, :, :, zq * fine : (zq + 1) * fine] = placed[:, i * fine : (i + 1) * fine].reshape(
                    PAD, bricks, fine
                )

    def plane(i):
        return feat[:, i * FACE : (i + 1) * FACE, :].reshape(bricks * FACE, fine)

    place(0, bricks, jnp.concatenate([plane(i) for i in range(EDGE)], axis=1), range(1, EDGE + 1))
    place(-1, bricks, plane(EDGE - 1), [0])
    place(1, bricks, plane(0), [EDGE + 1])

    loads[5].wait()
    for z in range(EDGE):
        for bc in range(TAPS2):
            at = bc * reach + z * fine
            wt[z * wide : (z + 1) * wide, at : at + 3 * fine] = wf[:, bc * 3 * fine : (bc + 1) * 3 * fine]

    def cube(x, b):
        return pbuf[x, b : b + EDGE].reshape(line, reach)

    parts = []
    for a in range(3):
        for b in range(3):
            parts.append(jnp.concatenate([cube(x + a, b) for x in range(EDGE)], axis=0))
    total = lax.dot_general(jnp.concatenate(parts, axis=1), wt[...], NT, preferred_element_type=F32)
    part_h[0] = total[0:line]
    part_h[1] = total[(EDGE - 1) * line :]
    for x in range(1, EDGE - 1):
        g_buf[me, x + 1] = jnp.maximum(total[x * line : (x + 1) * line], 0.0).astype(BF)

    def finish(k, a, first, x, xq):
        place(a, first, fh[k].reshape(bricks * FACE, fine), [xq])
        taps = wt[:, (a + 1) * 3 * reach : (a + 2) * 3 * reach]
        rest = lax.dot_general(
            jnp.concatenate([cube(xq, b) for b in range(3)], axis=1), taps, NT, preferred_element_type=F32
        )
        g_buf[me, x + 1] = jnp.maximum(part_h[k] + rest, 0.0).astype(BF)

    spans = ((2, EDGE - 2), (EDGE, 1), (1, 1))

    def hid_copy(j, k, chan):
        ref = g_buf.at[me, pl.ds(*spans[j])]
        return rc(ref, ref, s2.at[j, k], r2.at[j, me], sp, chan)

    def hid_wait(j):
        for k in range(1, n_chan):
            src = lax.rem(me + k, n_chan)
            ref = g_buf.at[src, pl.ds(*spans[j])]
            rc(ref, ref, s2.at[j, 0], r2.at[j, src], sp, src).wait_recv()

    for k, chan in enumerate(peers):
        hid_copy(0, k, chan).start()

    @pl.when(has_next)
    def _():
        dn_feat.wait_recv()

    finish(1, 1, 2 * bricks, EDGE - 1, EDGE + 1)
    for k, chan in enumerate(peers):
        hid_copy(1, k, chan).start()

    @pl.when(has_next)
    def _():
        for chan in range(n_chan):
            rc(g_buf.at[me, EDGE], g_buf.at[me, 0], hs2.at[chan], hr2.at[me], sp + 1, chan).start()

    @pl.when(has_prev)
    def _():
        up_feat.wait_recv()

    finish(0, -1, 0, 0, 0)
    for k, chan in enumerate(peers):
        hid_copy(2, k, chan).start()

    @pl.when(has_next)
    def _():
        dn_meta.wait_recv()

    @pl.when(has_prev)
    def _():
        up_meta.wait_recv()

    lanes = meta.shape[1]
    lane_par = jnp.where(
        iota((lanes, parents * cells), 1) // cells == iota((lanes, parents * cells), 0), 1.0, 0.0
    )

    def dest_table(k):
        block = meta[...] if k == 1 else mh[k // 2]
        rel = jnp.dot(block.astype(F32), lane_par, preferred_element_type=F32)[1:2].astype(jnp.int32)
        slot = rel - (2 - k) * slots
        target = slot * cells + iota((1, parents * cells), 1) % cells
        ids = iota((slots * cells, parents * cells), 0)
        ohd[k] = one(ids == jnp.where((slot >= 0) & (slot < slots), target, -1))

    n_own = HALF**3 * bricks
    spread = jnp.where(iota((lanes, n_own), 1) % bricks == iota((lanes, n_own), 0), 1.0, 0.0)

    def codes(block, n):
        code = jnp.dot(block.astype(F32), spread[:, 0:n], preferred_element_type=F32)[0:1].astype(jnp.int32)
        return code % 2, code // 2 % SLAB_Y, code // (2 * SLAB_Y)

    def wants(n, bc):
        at = iota((CLAYER, n), 0)
        par, yz = at // FACE, at % FACE
        y = par // (SLAB_Z // 2) * EDGE + yz // EDGE + bc // 3 - 1
        z = par % (SLAB_Z // 2) * EDGE + yz % EDGE + bc % 3 - 1
        return jnp.where((y >= 0) & (y < CY) & (z >= 0) & (z < CZ), y * CZ + z, FAR)

    x_bit, y_at, z_at = codes(meta[...], n_own)
    sub = iota((1, n_own), 1) // bricks
    key = (2 * y_at + sub % HALF) * CZ + 2 * z_at + sub // (HALF * HALF)
    layer = 2 * x_bit + sub // HALF % HALF
    for bc in range(TAPS2):
        want = wants(n_own, bc)
        for x in range(CX):
            hot_e[x, bc * CLAYER : (bc + 1) * CLAYER] = one(want == jnp.where(layer == x, key, -1))

    n_out = HALF * HALF * bricks
    for k in range(2):
        x_bit, y_at, z_at = codes(mh[k], n_out)
        sub = iota((1, n_out), 1) // bricks
        key = (2 * y_at + sub % HALF) * CZ + 2 * z_at + sub // HALF
        key = jnp.where(x_bit == 1 - k, key, -1)
        for bc in range(TAPS2):
            hot_o[k, bc * CLAYER : (bc + 1) * CLAYER] = one(wants(n_out, bc) == key)

    for k in range(3):
        dest_table(k)

    for load in loads[6:8]:
        load.wait()

    for j in range(3):
        hid_wait(j)

    def unpack(first, number):
        joined = jnp.concatenate(
            [g_buf[s, first : first + number].reshape(number * line, group) for s in range(n_chan)], axis=1
        )
        return pick(joined, perm[...]).astype(BF)

    full = EDGE * fine
    moved = unpack(1, EDGE)
    for x in range(EDGE):
        qbuf[x + 1, 1:LOW, :, fine : LOW * fine] = moved[x * line : (x + 1) * line].reshape(EDGE, bricks, full)

    def hot_rows(a, c, n):
        col = iota((bricks, n), 1)
        rows = []
        for yq in range(LOW):
            b, sy = source(yq)
            where = loc_of(a, b, c)
            where = jnp.where(where >= bricks, where - bricks, where + line) + sy * bricks
            rows.append(one(col == where))
        return jnp.concatenate(rows, axis=0)

    tail = fine * (EDGE - 1)
    edge_y = pick(
        one(iota((bricks, bricks), 1) == loc_of(0, -1, 0) - bricks),
        jnp.concatenate([moved[x * line + line - bricks : (x + 1) * line] for x in range(EDGE)], axis=1),
    ).astype(BF)
    edge_z = pick(
        hot_rows(0, -1, line), jnp.concatenate([moved[x * line : (x + 1) * line, tail:] for x in range(EDGE)], axis=1)
    ).astype(BF)
    for x in range(EDGE):
        qbuf[x + 1, 0, :, fine : LOW * fine] = edge_y[:, x * full : (x + 1) * full]
        qbuf[x + 1, :, :, 0:fine] = edge_z[:, x * fine : (x + 1) * fine].reshape(LOW, bricks, fine)

    @pl.when(has_prev)
    def _():
        for chan in range(n_chan):
            rc(g_buf.at[chan, 0], g_buf.at[chan, 0], hs2.at[chan], hr2.at[chan], sp - 1, chan).wait_recv()

    joint = jnp.concatenate([moved[tail // fine * line :], unpack(0, 1)], axis=0)
    qbuf[0, :, :, fine : LOW * fine] = pick(hot_rows(-1, 0, 2 * line), joint).astype(BF).reshape(LOW, bricks, full)
    qbuf[0, :, :, 0:fine] = pick(hot_rows(-1, -1, 2 * line), joint[:, tail:]).astype(BF).reshape(LOW, bricks, fine)

    stacked = []
    for qz in range(HALF):
        for qx in range(HALF):
            for qy in range(HALF):
                stacked.append(
                    jnp.concatenate(
                        [
                            qbuf[2 * qx + a, 2 * qy + b, :, 2 * qz * fine : (2 * qz + 3) * fine]
                            for a in range(3)
                            for b in range(3)
                        ],
                        axis=1,
                    )
                )
    pieces = lax.dot_general(jnp.concatenate(stacked, axis=0), wd[...], NT, preferred_element_type=F32)
    pieces = jnp.maximum(pieces, 0.0)
    part = 2 * side
    c_buf[me] = jnp.concatenate([pieces[h * part : (h + 1) * part] for h in range(HALF)], axis=1).astype(BF)

    for k, chan in enumerate(peers):
        rc(c_buf.at[me], c_buf.at[me], s3.at[k], r3.at[me], sp, chan).start()

    @pl.when(has_next)
    def _():
        for chan in range(n_chan):
            rc(c_buf.at[me, pl.ds(side, side)], cp.at[me], hs3.at[0, chan], hr3.at[0, me], sp + 1, chan).start()

    @pl.when(has_prev)
    def _():
        for chan in range(n_chan):
            rc(c_buf.at[me, pl.ds(0, side)], cn.at[me], hs3.at[1, chan], hr3.at[1, me], sp - 1, chan).start()

    for load in loads[8:]:
        load.wait()
    own = gain.shape[1]
    gain_col = jnp.sum(
        jnp.where(iota((own, own), 0) == iota((own, own), 1), gain[...], 0.0), axis=1, keepdims=True
    )

    for k in range(1, n_chan):
        src = lax.rem(me + k, n_chan)
        rc(c_buf.at[src], c_buf.at[src], s3.at[0], r3.at[src], sp, src).wait_recv()

    def all_channels(buf):
        return jnp.concatenate(
            [
                jnp.concatenate([buf[s][:, h * own_d : (h + 1) * own_d] for s in range(n_chan)], axis=1)
                for h in range(HALF)
            ],
            axis=0,
        )

    def coarse_taps(a):
        blocks = []
        for bc in range(TAPS2):
            blocks.append(
                jnp.concatenate(
                    [
                        e_buf[x + a, bc * CLAYER + g * FACE : bc * CLAYER + (g + 1) * FACE, :]
                        for g in range(parents)
                        for x in range(CX)
                    ],
                    axis=0,
                )
            )
        span = TAPS2 * coarse
        taps = wc[:, a * span : (a + 1) * span]
        return lax.dot_general(taps, jnp.concatenate(blocks, axis=1), NT, preferred_element_type=F32)

    inside = all_channels(c_buf)
    for x in range(CX):
        e_buf[x + 1] = pick(hot_e[x], inside).astype(BF)
    total = coarse_taps(1)

    @pl.when(has_prev)
    def _():
        for chan in range(n_chan):
            rc(cp.at[chan], cp.at[chan], hs3.at[0, chan], hr3.at[0, chan], sp - 1, chan).wait_recv()

    @pl.when(has_next)
    def _():
        for chan in range(n_chan):
            rc(cn.at[chan], cn.at[chan], hs3.at[1, chan], hr3.at[1, chan], sp + 1, chan).wait_recv()

    e_buf[0] = pick(hot_o[0], all_channels(cp)).astype(BF)
    e_buf[CX + 1] = pick(hot_o[1], all_channels(cn)).astype(BF)
    total = total + coarse_taps(0) + coarse_taps(2)
    rounded = total.astype(BF)
    pb[1] = rounded
    values = rounded.astype(F32)
    pw[1, me] = jnp.sum(values * values, axis=0, keepdims=True)

    for k, chan in enumerate(peers):
        rc(pw.at[1, me], pw.at[1, me], ws4.at[1, k], wr4.at[1, me], sp, chan).start()

    @pl.when(has_next)
    def _():
        rc(pb.at[1], pb.at[0], s4.at[0], r4.at[0], sp + 1, me).start()
        for chan in range(n_chan):
            rc(pw.at[1, me], pw.at[0, me], ws4.at[0, chan], wr4.at[0, me], sp + 1, chan).start()

    @pl.when(has_prev)
    def _():
        rc(pb.at[1], pb.at[2], s4.at[1], r4.at[1], sp - 1, me).start()
        for chan in range(n_chan):
            rc(pw.at[1, me], pw.at[2, me], ws4.at[2, chan], wr4.at[2, me], sp - 1, chan).start()

    def normed(k):
        power = pw[k, 0]
        for s in range(1, n_chan):
            power = power + pw[k, s]
        scaled = pb[k].astype(F32) * lax.rsqrt(power / coarse + epsilon) * gain_col
        return lax.dot_general(scaled.astype(BF), ohd[k], NT, preferred_element_type=F32)

    for k in range(1, n_chan):
        src = lax.rem(me + k, n_chan)
        rc(pw.at[1, src], pw.at[1, src], ws4.at[1, 0], wr4.at[1, src], sp, src).wait_recv()
    result = normed(1)

    @pl.when(has_prev)
    def _():
        rc(pb.at[0], pb.at[0], s4.at[0], r4.at[0], sp - 1, me).wait_recv()
        for chan in range(n_chan):
            rc(pw.at[0, chan], pw.at[0, chan], ws4.at[0, chan], wr4.at[0, chan], sp - 1, chan).wait_recv()

    @pl.when(has_next)
    def _():
        rc(pb.at[2], pb.at[2], s4.at[1], r4.at[1], sp + 1, me).wait_recv()
        for chan in range(n_chan):
            rc(pw.at[2, chan], pw.at[2, chan], ws4.at[2, chan], wr4.at[2, chan], sp + 1, chan).wait_recv()

    out[...] = (result + normed(0) + normed(2)).astype(BF)

    for k, chan in enumerate(peers):
        for j in range(3):
            hid_copy(j, k, chan).wait_send()
        rc(c_buf.at[me], c_buf.at[me], s3.at[k], r3.at[me], sp, chan).wait_send()
        rc(pw.at[1, me], pw.at[1, me], ws4.at[1, k], wr4.at[1, me], sp, chan).wait_send()

    @pl.when(has_next)
    def _():
        up_meta.wait_send()
        up_feat.wait_send()
        rc(pb.at[1], pb.at[0], s4.at[0], r4.at[0], sp + 1, me).wait_send()
        for chan in range(n_chan):
            rc(g_buf.at[me, EDGE], g_buf.at[me, 0], hs2.at[chan], hr2.at[me], sp + 1, chan).wait_send()
            rc(c_buf.at[me, pl.ds(side, side)], cp.at[me], hs3.at[0, chan], hr3.at[0, me], sp + 1, chan).wait_send()
            rc(pw.at[1, me], pw.at[0, me], ws4.at[0, chan], wr4.at[0, me], sp + 1, chan).wait_send()

    @pl.when(has_prev)
    def _():
        dn_meta.wait_send()
        dn_feat.wait_send()
        rc(pb.at[1], pb.at[2], s4.at[1], r4.at[1], sp - 1, me).wait_send()
        for chan in range(n_chan):
            rc(c_buf.at[me, pl.ds(0, side)], cn.at[me], hs3.at[1, chan], hr3.at[1, me], sp - 1, chan).wait_send()
            rc(pw.at[1, me], pw.at[2, me], ws4.at[2, chan], wr4.at[2, me], sp - 1, chan).wait_send()


def body(n_space, n_chan, features, neighbours, parent_index, octant, parent_dest, conv_fine, conv_down, conv_coarse, norm_gain):
    bricks, _, fine = features.shape
    parents = parent_dest.shape[0]
    slots = 2 * parents
    own_d = conv_down.shape[0]
    own = conv_coarse.shape[0]
    cells = EDGE**3
    coarse = own_d * n_chan
    group = EDGE * fine // n_chan
    vmem = pl.BlockSpec(memory_space=pltpu.VMEM)
    hbm = pl.BlockSpec(memory_space=pltpu.HBM)
    dma = pltpu.SemaphoreType.DMA

    def fixed(x):
        return pltpu.with_memory_space_constraint(x, pltpu.HBM)

    return pl.pallas_call(
        functools.partial(fused_kernel, n_space, n_chan, bricks, slots),
        out_shape=jax.ShapeDtypeStruct((own, slots * cells), BF),
        in_specs=[hbm] * 10,
        out_specs=vmem,
        scratch_shapes=[
            pltpu.VMEM(features.shape, BF),
            pltpu.VMEM(neighbours.shape, jnp.int32),
            pltpu.VMEM(conv_fine.shape, BF),
            pltpu.VMEM((group, TAPS2 * PAD * fine), BF),
            pltpu.VMEM((1, own), F32),
            pltpu.VMEM((1, bricks), jnp.int32),
            pltpu.VMEM((1, bricks), jnp.int32),
            pltpu.VMEM((1, parents), jnp.int32),
            pltpu.VMEM((8, 128), jnp.int32),
            pltpu.VMEM(conv_down.shape, BF),
            pltpu.VMEM(conv_coarse.shape, BF),
            pltpu.VMEM((n_chan * group, n_chan * group), BF),
            pltpu.VMEM((2, bricks, FACE, fine), BF),
            pltpu.VMEM((2, 8, 128), jnp.int32),
            pltpu.VMEM((PAD, PAD, bricks, PAD * fine), BF),
            pltpu.VMEM((2, EDGE * bricks, group), F32),
            pltpu.VMEM((n_chan, LOW, EDGE * bricks, group), BF),
            pltpu.VMEM((LOW, LOW, bricks, LOW * fine), BF),
            pltpu.VMEM((n_chan, HALF * HALF * bricks, HALF * own_d), BF),
            pltpu.VMEM((n_chan, HALF * bricks, HALF * own_d), BF),
            pltpu.VMEM((n_chan, HALF * bricks, HALF * own_d), BF),
            pltpu.VMEM((CX + 2, TAPS2 * CLAYER, coarse), BF),
            pltpu.VMEM((CX, TAPS2 * CLAYER, HALF**3 * bricks), BF),
            pltpu.VMEM((2, TAPS2 * CLAYER, HALF**2 * bricks), BF),
            pltpu.VMEM((3, own, parents * cells), BF),
            pltpu.VMEM((3, n_chan, 1, parents * cells), F32),
            pltpu.VMEM((3, slots * cells, parents * cells), BF),
            dma((10,)),
            dma((2, 2)),
            dma((2, 2)),
            dma((3, n_chan - 1)),
            dma((3, n_chan)),
            dma((n_chan,)),
            dma((n_chan,)),
            dma((n_chan - 1,)),
            dma((n_chan,)),
            dma((2, n_chan)),
            dma((2, n_chan)),
            dma((2,)),
            dma((2,)),
            dma((3, n_chan)),
            dma((3, n_chan)),
        ],
        compiler_params=pltpu.CompilerParams(
            collective_id=0, has_side_effects=True, vmem_limit_bytes=40000000
        ),
    )(
        fixed(features),
        fixed(neighbours),
        fixed(parent_index.reshape(1, -1)),
        fixed(octant.reshape(1, -1)),
        fixed(parent_dest.reshape(1, -1)),
        fixed(conv_fine),
        fixed(conv_down),
        fixed(conv_coarse),
        fixed(norm_gain.reshape(1, -1)),
        fixed(table(n_chan, fine)),
    )


def solution(mesh):
    sizes = dict(mesh.shape)
    return jax.shard_map(
        functools.partial(body, sizes["space"], sizes["chan"]),
        mesh=mesh,
        in_specs=(
            P("space", None, None),
            P("space", None),
            P("space"),
            P("space"),
            P("space"),
            P("chan", None),
            P("chan", None),
            P("chan", None),
            P("chan"),
        ),
        out_specs=P("chan", "space"),
        check_vma=False,
    )
```

```python
import functools

import jax
import jax.numpy as jnp
import numpy as np
from jax import lax
from jax.experimental import pallas as pl
from jax.experimental.pallas import tpu as pltpu
from jax.sharding import PartitionSpec as P

EDGE = 4
SLAB_Y = 4
SLAB_Z = 4
PAD = EDGE + 2
LOW = EDGE + 1
HALF = EDGE // 2
FACE = EDGE * EDGE
CY = SLAB_Y * HALF
CZ = SLAB_Z * HALF
CLAYER = CY * CZ
CX = 2 * HALF
TAPS2 = 9
epsilon = 1e-06
FAR = 1 << 20
BF = jnp.bfloat16
F32 = jnp.float32
NT = (((1,), (1,)), ((), ()))


def iota(shape, dim):
    return lax.broadcasted_iota(jnp.int32, shape, dim)


def one(cond):
    return jnp.where(cond, 1.0, 0.0).astype(BF)


def pick(a, b):
    return jnp.dot(a, b, preferred_element_type=F32)


def tap2(b, c):
    return 3 * (b + 1) + c + 1


def source(pos):
    if pos == 0:
        return -1, EDGE - 1
    if pos == EDGE + 1:
        return 1, 0
    return 0, pos - 1


def table(n_chan, fine):
    wide = fine // n_chan
    r = np.arange(n_chan * EDGE * wide)[:, None]
    q = np.arange(n_chan * EDGE * wide)[None, :]
    group = EDGE * wide
    perm = (r % group) // wide * fine + r // group * wide + r % wide == q
    return jnp.asarray(np.asarray(perm, np.float32).astype(jnp.bfloat16))


def fused_kernel(
    n_space, n_chan, bricks, slots,
    feat_hbm, nbr_hbm, parent_hbm, octant_hbm, dest_hbm, wf_hbm, wd_hbm, wc_hbm, gain_hbm, perm_hbm,
    out,
    feat, nbr, wf, wt, gain, parent_in, octant_in, dest_in, meta, wd, wc, perm,
    fh, mh, pbuf, part_h, g_buf, qbuf, c_buf, cp, cn, e_buf, hot_e, hot_o, acc, pb, pw, ohd,
    wsem, s1, r1, s2, r2, hs2, hr2, s3, r3, hs3, hr3, s4, r4, ws4, wr4,
):
    sp = lax.axis_index("space")
    me = lax.axis_index("chan")
    has_prev = sp > 0
    has_next = sp < n_space - 1
    fine = feat.shape[2]
    wide = fine // n_chan
    parents = dest_in.shape[1]
    cells = EDGE**3
    own_d = wd.shape[0]
    coarse = own_d * n_chan
    group = EDGE * wide
    line = EDGE * bricks
    side = HALF * bricks

    def rc(src, dst, ss, rs, space, chan):
        return pltpu.make_async_remote_copy(
            src_ref=src,
            dst_ref=dst,
            send_sem=ss,
            recv_sem=rs,
            device_id={"space": space, "chan": chan},
            device_id_type=pl.DeviceIdType.MESH,
        )

    peers = [lax.rem(me + k, n_chan) for k in range(1, n_chan)]
    barrier = pltpu.get_barrier_semaphore()

    def greet(space, chan):
        pl.semaphore_signal(
            barrier,
            inc=1,
            device_id={"space": space, "chan": chan},
            device_id_type=pl.DeviceIdType.MESH,
        )

    @pl.when(has_prev)
    def _():
        greet(sp - 1, me)

    @pl.when(has_next)
    def _():
        greet(sp + 1, me)

    for chan in peers:
        greet(sp, chan)

    loads = [
        pltpu.make_async_copy(src, dst, wsem.at[k])
        for k, (src, dst) in enumerate(
            (
                (nbr_hbm, nbr),
                (feat_hbm, feat),
                (parent_hbm, parent_in),
                (octant_hbm, octant_in),
                (dest_hbm, dest_in),
                (wf_hbm, wf),
                (perm_hbm, perm),
                (wd_hbm, wd),
                (gain_hbm, gain),
                (wc_hbm, wc),
            )
        )
    ]
    for load in loads:
        load.start()

    up_feat = rc(feat_hbm.at[:, pl.ds((EDGE - 1) * FACE, FACE), :], fh.at[0], s1.at[0, 0], r1.at[0, 0], sp + 1, me)
    up_meta = rc(meta, mh.at[0], s1.at[0, 1], r1.at[0, 1], sp + 1, me)
    dn_feat = rc(feat_hbm.at[:, pl.ds(0, FACE), :], fh.at[1], s1.at[1, 0], r1.at[1, 0], sp - 1, me)
    dn_meta = rc(meta, mh.at[1], s1.at[1, 1], r1.at[1, 1], sp - 1, me)

    pl.semaphore_wait(barrier, n_chan - 1 + has_prev.astype(jnp.int32) + has_next.astype(jnp.int32))

    @pl.when(has_next)
    def _():
        up_feat.start()

    @pl.when(has_prev)
    def _():
        dn_feat.start()

    @pl.when(jnp.logical_not(has_prev))
    def _():
        fh[0] = jnp.zeros(fh.shape[1:], BF)
        mh[0] = jnp.zeros(mh.shape[1:], jnp.int32)
        for s in range(n_chan):
            g_buf[s, 0] = jnp.zeros(g_buf.shape[2:], BF)
        cp[...] = jnp.zeros(cp.shape, BF)
        pb[0] = jnp.zeros(pb.shape[1:], BF)
        pw[0] = jnp.zeros(pw.shape[1:], F32)

    @pl.when(jnp.logical_not(has_next))
    def _():
        fh[1] = jnp.zeros(fh.shape[1:], BF)
        mh[1] = jnp.zeros(mh.shape[1:], jnp.int32)
        cn[...] = jnp.zeros(cn.shape, BF)
        pb[2] = jnp.zeros(pb.shape[1:], BF)
        pw[2] = jnp.zeros(pw.shape[1:], F32)

    reach = PAD * fine
    for z in range(EDGE):
        for bc in range(TAPS2):
            at = bc * reach
            rows = slice(z * wide, (z + 1) * wide)
            if z > 0:
                wt[rows, at : at + z * fine] = jnp.zeros((wide, z * fine), BF)
            if z < EDGE - 1:
                wt[rows, at + (z + 3) * fine : at + reach] = jnp.zeros((wide, (EDGE - 1 - z) * fine), BF)
    meta[...] = jnp.zeros(meta.shape, jnp.int32)

    for load in loads[2:5]:
        load.wait()
    local = parent_in[...] - sp * parents
    octant = octant_in[...]
    y_pos = 2 * (local // (SLAB_Z // 2)) + octant // 2 % 2
    z_pos = 2 * (local % (SLAB_Z // 2)) + octant // 4
    meta[0:1, 0:bricks] = octant % 2 + 2 * y_pos + 2 * SLAB_Y * z_pos
    meta[1:2, 0:parents] = dest_in[...] - (sp - 1) * slots

    @pl.when(has_next)
    def _():
        up_meta.start()

    @pl.when(has_prev)
    def _():
        dn_meta.start()

    for load in loads[0:2]:
        load.wait()
    raw = nbr[...]
    loc = jnp.where(raw >= 0, raw - bricks * (sp - 1), -FAR)
    here = iota((bricks, 1), 0) + bricks

    def loc_of(a, b, c):
        k = 9 * (a + 1) + tap2(b, c)
        if k == 13:
            return here
        k = k - (k > 13)
        return loc[:, k : k + 1]

    def place(a, first, sources, planes):
        wide_k = sources.shape[0]
        col = iota((bricks, wide_k), 1)
        keys = {
            (b, c): jnp.broadcast_to((loc_of(a, b, c) - first) * FACE, (bricks, wide_k))
            for b in (-1, 0, 1)
            for c in (-1, 0, 1)
        }
        for zq in range(PAD):
            c, sz = source(zq)
            hots = []
            for yq in range(PAD):
                b, sy = source(yq)
                hots.append(one(col == keys[b, c] + (sy * EDGE + sz)))
            placed = pick(jnp.concatenate(hots, axis=0), sources).astype(BF)
            for i, xq in enumerate(planes):
                pbuf[xq, :, :, zq * fine : (zq + 1) * fine] = placed[:, i * fine : (i + 1) * fine].reshape(
                    PAD, bricks, fine
                )

    def plane(i):
        return feat[:, i * FACE : (i + 1) * FACE, :].reshape(bricks * FACE, fine)

    place(0, bricks, jnp.concatenate([plane(i) for i in range(EDGE)], axis=1), range(1, EDGE + 1))
    place(-1, bricks, plane(EDGE - 1), [0])
    place(1, bricks, plane(0), [EDGE + 1])

    loads[5].wait()
    for z in range(EDGE):
        for bc in range(TAPS2):
            at = bc * reach + z * fine
            wt[z * wide : (z + 1) * wide, at : at + 3 * fine] = wf[:, bc * 3 * fine : (bc + 1) * 3 * fine]

    def cube(x, b):
        return pbuf[x, b : b + EDGE].reshape(line, reach)

    parts = []
    for a in range(3):
        for b in range(3):
            parts.append(jnp.concatenate([cube(x + a, b) for x in range(EDGE)], axis=0))
    total = lax.dot_general(jnp.concatenate(parts, axis=1), wt[...], NT, preferred_element_type=F32)
    part_h[0] = total[0:line]
    part_h[1] = total[(EDGE - 1) * line :]
    for x in range(1, EDGE - 1):
        g_buf[me, x + 1] = jnp.maximum(total[x * line : (x + 1) * line], 0.0).astype(BF)

    def rest(a, xq):
        taps = wt[:, (a + 1) * 3 * reach : (a + 2) * 3 * reach]
        return lax.dot_general(
            jnp.concatenate([cube(xq, b) for b in range(3)], axis=1), taps, NT, preferred_element_type=F32
        )

    spans = ((2, EDGE - 2), (EDGE, 1), (1, 1))

    def hid_copy(j, k, chan):
        ref = g_buf.at[me, pl.ds(*spans[j])]
        return rc(ref, ref, s2.at[j, k], r2.at[j, me], sp, chan)

    def hid_wait(j):
        for k in range(1, n_chan):
            src = lax.rem(me + k, n_chan)
            ref = g_buf.at[src, pl.ds(*spans[j])]
            rc(ref, ref, s2.at[j, 0], r2.at[j, src], sp, src).wait_recv()

    for k, chan in enumerate(peers):
        hid_copy(0, k, chan).start()

    @pl.when(has_next)
    def _():
        dn_feat.wait_recv()

    @pl.when(has_prev)
    def _():
        up_feat.wait_recv()

    place(1, 2 * bricks, fh[1].reshape(bricks * FACE, fine), [EDGE + 1])
    place(-1, 0, fh[0].reshape(bricks * FACE, fine), [0])
    g_buf[me, EDGE] = jnp.maximum(part_h[1] + rest(1, EDGE + 1), 0.0).astype(BF)
    g_buf[me, 1] = jnp.maximum(part_h[0] + rest(-1, 0), 0.0).astype(BF)
    for j in (1, 2):
        for k, chan in enumerate(peers):
            hid_copy(j, k, chan).start()

    twin = me + 1 - 2 * lax.rem(me, 2)
    spread_to = [lax.rem(c + 2 * j, n_chan) for j in range(n_chan // 2) for c in (me, twin)]

    def hid_halo(k):
        return rc(g_buf.at[me, EDGE], g_buf.at[me, 0], hs2.at[k], hr2.at[me], sp + 1, spread_to[k])

    @pl.when(has_next)
    def _():
        for k in range(n_chan):
            hid_halo(k).start()

    @pl.when(has_next)
    def _():
        dn_meta.wait_recv()

    @pl.when(has_prev)
    def _():
        up_meta.wait_recv()

    lanes = meta.shape[1]
    lane_par = jnp.where(
        iota((lanes, parents * cells), 1) % CLAYER // FACE == iota((lanes, parents * cells), 0), 1.0, 0.0
    )

    def dest_table(k):
        block = meta[...] if k == 1 else mh[k // 2]
        rel = jnp.dot(block.astype(F32), lane_par, preferred_element_type=F32)[1:2].astype(jnp.int32)
        slot = rel - (2 - k) * slots
        at = iota((1, parents * cells), 1)
        target = slot * cells + at // CLAYER * FACE + at % FACE
        ids = iota((slots * cells, parents * cells), 0)
        ohd[k] = one(ids == jnp.where((slot >= 0) & (slot < slots), target, -1))

    n_own = HALF**3 * bricks
    spread = jnp.where(iota((lanes, n_own), 1) % bricks == iota((lanes, n_own), 0), 1.0, 0.0)

    def codes(block, n):
        code = jnp.dot(block.astype(F32), spread[:, 0:n], preferred_element_type=F32)[0:1].astype(jnp.int32)
        return code % 2, code // 2 % SLAB_Y, code // (2 * SLAB_Y)

    def wants(n, bc):
        at = iota((CLAYER, n), 0)
        par, yz = at // FACE, at % FACE
        y = par // (SLAB_Z // 2) * EDGE + yz // EDGE + bc // 3 - 1
        z = par % (SLAB_Z // 2) * EDGE + yz % EDGE + bc % 3 - 1
        return jnp.where((y >= 0) & (y < CY) & (z >= 0) & (z < CZ), y * CZ + z, FAR)

    x_bit, y_at, z_at = codes(meta[...], n_own)
    sub = iota((1, n_own), 1) // bricks
    key = (2 * y_at + sub % HALF) * CZ + 2 * z_at + sub // (HALF * HALF)
    layer = 2 * x_bit + sub // HALF % HALF
    for bc in range(TAPS2):
        want = wants(n_own, bc)
        for x in range(CX):
            hot_e[x, bc * CLAYER : (bc + 1) * CLAYER] = one(want == jnp.where(layer == x, key, -1))

    n_out = HALF * HALF * bricks
    for k in range(2):
        x_bit, y_at, z_at = codes(mh[k], n_out)
        sub = iota((1, n_out), 1) // bricks
        key = (2 * y_at + sub % HALF) * CZ + 2 * z_at + sub // HALF
        key = jnp.where(x_bit == 1 - k, key, -1)
        for bc in range(TAPS2):
            hot_o[k, bc * CLAYER : (bc + 1) * CLAYER] = one(wants(n_out, bc) == key)

    for k in range(3):
        dest_table(k)

    for load in loads[6:8]:
        load.wait()

    hid_wait(0)

    full = EDGE * fine
    tail = fine * (EDGE - 1)

    def unpack(at):
        joined = jnp.concatenate(
            [jnp.concatenate([g_buf[s, x + 1] for s in range(n_chan)], axis=1) for x in at], axis=0
        )
        moved = pick(joined, perm[...]).astype(BF)
        return [moved[i * line : (i + 1) * line] for i in range(len(at))]

    def hot_rows(a, c, n):
        col = iota((bricks, n), 1)
        rows = []
        for yq in range(LOW):
            b, sy = source(yq)
            where = loc_of(a, b, c)
            where = jnp.where(where >= bricks, where - bricks, where + line) + sy * bricks
            rows.append(one(col == where))
        return jnp.concatenate(rows, axis=0)

    def lay_out(at):
        moved = unpack(at)
        edge_y = pick(
            one(iota((bricks, bricks), 1) == loc_of(0, -1, 0) - bricks),
            jnp.concatenate([m[line - bricks :] for m in moved], axis=1),
        ).astype(BF)
        edge_z = pick(hot_rows(0, -1, line), jnp.concatenate([m[:, tail:] for m in moved], axis=1)).astype(BF)
        for i, x in enumerate(at):
            qbuf[x + 1, 1:LOW, :, fine : LOW * fine] = moved[i].reshape(EDGE, bricks, full)
            qbuf[x + 1, 0, :, fine : LOW * fine] = edge_y[:, i * full : (i + 1) * full]
            qbuf[x + 1, :, :, 0:fine] = edge_z[:, i * fine : (i + 1) * fine].reshape(LOW, bricks, fine)
        return moved

    lay_out(list(range(1, EDGE - 1)))

    for j in (1, 2):
        hid_wait(j)

    def down(qx):
        stacked = []
        for qz in range(HALF):
            for qy in range(HALF):
                stacked.append(
                    jnp.concatenate(
                        [
                            qbuf[2 * qx + a, 2 * qy + b, :, 2 * qz * fine : (2 * qz + 3) * fine]
                            for a in range(3)
                            for b in range(3)
                        ],
                        axis=1,
                    )
                )
        pieces = lax.dot_general(jnp.concatenate(stacked, axis=0), wd[...], NT, preferred_element_type=F32)
        pieces = jnp.maximum(pieces, 0.0)
        c_buf[me, qx * side : (qx + 1) * side] = jnp.concatenate(
            [pieces[h * side : (h + 1) * side] for h in range(HALF)], axis=1
        ).astype(BF)

    def part_copy(qx, k, chan):
        ref = c_buf.at[me, pl.ds(qx * side, side)]
        return rc(ref, ref, s3.at[qx, k], r3.at[qx, me], sp, chan)

    def up_part(k):
        return rc(c_buf.at[me, pl.ds(side, side)], cp.at[me], hs3.at[0, k], hr3.at[0, me], sp + 1, spread_to[k])

    def dn_part(k):
        return rc(c_buf.at[me, pl.ds(0, side)], cn.at[me], hs3.at[1, k], hr3.at[1, me], sp - 1, spread_to[k])

    last = lay_out([0, EDGE - 1])[1]
    down(1)
    for k, chan in enumerate(peers):
        part_copy(1, k, chan).start()

    @pl.when(has_next)
    def _():
        for k in range(n_chan):
            up_part(k).start()

    @pl.when(has_prev)
    def _():
        for chan in range(n_chan):
            rc(g_buf.at[chan, 0], g_buf.at[chan, 0], hs2.at[chan], hr2.at[chan], sp - 1, chan).wait_recv()

    joint = jnp.concatenate(
        [last, pick(jnp.concatenate([g_buf[s, 0] for s in range(n_chan)], axis=1), perm[...]).astype(BF)], axis=0
    )
    qbuf[0, :, :, fine : LOW * fine] = pick(hot_rows(-1, 0, 2 * line), joint).astype(BF).reshape(LOW, bricks, full)
    qbuf[0, :, :, 0:fine] = pick(hot_rows(-1, -1, 2 * line), joint[:, tail:]).astype(BF).reshape(LOW, bricks, fine)
    down(0)

    for k, chan in enumerate(peers):
        part_copy(0, k, chan).start()

    @pl.when(has_prev)
    def _():
        for k in range(n_chan):
            dn_part(k).start()

    for load in loads[8:]:
        load.wait()
    own = gain.shape[1]
    gain_col = jnp.sum(
        jnp.where(iota((own, own), 0) == iota((own, own), 1), gain[...], 0.0), axis=1, keepdims=True
    )

    for qx in range(HALF):
        for k in range(1, n_chan):
            src = lax.rem(me + k, n_chan)
            ref = c_buf.at[src, pl.ds(qx * side, side)]
            rc(ref, ref, s3.at[qx, 0], r3.at[qx, src], sp, src).wait_recv()

    def all_channels(buf):
        return jnp.concatenate(
            [
                jnp.concatenate([buf[s][:, h * own_d : (h + 1) * own_d] for s in range(n_chan)], axis=1)
                for h in range(HALF)
            ],
            axis=0,
        )

    def coarse_taps(a, at):
        blocks = []
        for bc in range(TAPS2):
            rows = slice(bc * CLAYER, (bc + 1) * CLAYER)
            blocks.append(jnp.concatenate([e_buf[x + a, rows] for x in at], axis=0))
        span = TAPS2 * coarse
        taps = wc[:, a * span : (a + 1) * span]
        return lax.dot_general(taps, jnp.concatenate(blocks, axis=1), NT, preferred_element_type=F32)

    inside = all_channels(c_buf)
    for x in range(CX):
        e_buf[x + 1] = pick(hot_e[x], inside).astype(BF)
    total = coarse_taps(1, range(CX))
    low = coarse_taps(0, range(1, CX))
    high = coarse_taps(2, range(CX - 1))
    acc[...] = total
    acc[:, CLAYER:] += low
    acc[:, : (CX - 1) * CLAYER] += high

    @pl.when(has_prev)
    def _():
        for chan in range(n_chan):
            rc(cp.at[chan], cp.at[chan], hs3.at[0, chan], hr3.at[0, chan], sp - 1, chan).wait_recv()

    @pl.when(has_next)
    def _():
        for chan in range(n_chan):
            rc(cn.at[chan], cn.at[chan], hs3.at[1, chan], hr3.at[1, chan], sp + 1, chan).wait_recv()

    e_buf[0] = pick(hot_o[0], all_channels(cp)).astype(BF)
    e_buf[CX + 1] = pick(hot_o[1], all_channels(cn)).astype(BF)
    low = coarse_taps(0, [0])
    high = coarse_taps(2, [CX - 1])
    total = acc[...]
    edge = (CX - 1) * CLAYER
    total = jnp.concatenate(
        [total[:, :CLAYER] + low, total[:, CLAYER:edge], total[:, edge:] + high], axis=1
    )
    rounded = total.astype(BF)
    pb[1] = rounded
    values = rounded.astype(F32)
    pw[1, me] = jnp.sum(values * values, axis=0, keepdims=True)

    for k, chan in enumerate(peers):
        rc(pw.at[1, me], pw.at[1, me], ws4.at[1, k], wr4.at[1, me], sp, chan).start()

    @pl.when(has_next)
    def _():
        rc(pb.at[1], pb.at[0], s4.at[0], r4.at[0], sp + 1, me).start()
        for chan in range(n_chan):
            rc(pw.at[1, me], pw.at[0, me], ws4.at[0, chan], wr4.at[0, me], sp + 1, chan).start()

    @pl.when(has_prev)
    def _():
        rc(pb.at[1], pb.at[2], s4.at[1], r4.at[1], sp - 1, me).start()
        for chan in range(n_chan):
            rc(pw.at[1, me], pw.at[2, me], ws4.at[2, chan], wr4.at[2, me], sp - 1, chan).start()

    def normed(k):
        power = pw[k, 0]
        for s in range(1, n_chan):
            power = power + pw[k, s]
        scaled = pb[k].astype(F32) * lax.rsqrt(power / coarse + epsilon) * gain_col
        return lax.dot_general(scaled.astype(BF), ohd[k], NT, preferred_element_type=F32)

    for k in range(1, n_chan):
        src = lax.rem(me + k, n_chan)
        rc(pw.at[1, src], pw.at[1, src], ws4.at[1, 0], wr4.at[1, src], sp, src).wait_recv()
    result = normed(1)

    @pl.when(has_prev)
    def _():
        rc(pb.at[0], pb.at[0], s4.at[0], r4.at[0], sp - 1, me).wait_recv()
        for chan in range(n_chan):
            rc(pw.at[0, chan], pw.at[0, chan], ws4.at[0, chan], wr4.at[0, chan], sp - 1, chan).wait_recv()

    @pl.when(has_next)
    def _():
        rc(pb.at[2], pb.at[2], s4.at[1], r4.at[1], sp + 1, me).wait_recv()
        for chan in range(n_chan):
            rc(pw.at[2, chan], pw.at[2, chan], ws4.at[2, chan], wr4.at[2, chan], sp + 1, chan).wait_recv()

    out[...] = (result + normed(0) + normed(2)).astype(BF)

    for k, chan in enumerate(peers):
        for j in range(3):
            hid_copy(j, k, chan).wait_send()
        for qx in range(HALF):
            part_copy(qx, k, chan).wait_send()
        rc(pw.at[1, me], pw.at[1, me], ws4.at[1, k], wr4.at[1, me], sp, chan).wait_send()

    @pl.when(has_next)
    def _():
        up_meta.wait_send()
        up_feat.wait_send()
        rc(pb.at[1], pb.at[0], s4.at[0], r4.at[0], sp + 1, me).wait_send()
        for chan in range(n_chan):
            hid_halo(chan).wait_send()
            up_part(chan).wait_send()
            rc(pw.at[1, me], pw.at[0, me], ws4.at[0, chan], wr4.at[0, me], sp + 1, chan).wait_send()

    @pl.when(has_prev)
    def _():
        dn_meta.wait_send()
        dn_feat.wait_send()
        rc(pb.at[1], pb.at[2], s4.at[1], r4.at[1], sp - 1, me).wait_send()
        for chan in range(n_chan):
            dn_part(chan).wait_send()
            rc(pw.at[1, me], pw.at[2, me], ws4.at[2, chan], wr4.at[2, me], sp - 1, chan).wait_send()


def body(n_space, n_chan, features, neighbours, parent_index, octant, parent_dest, conv_fine, conv_down, conv_coarse, norm_gain):
    bricks, _, fine = features.shape
    parents = parent_dest.shape[0]
    slots = 2 * parents
    own_d = conv_down.shape[0]
    own = conv_coarse.shape[0]
    cells = EDGE**3
    coarse = own_d * n_chan
    group = EDGE * fine // n_chan
    vmem = pl.BlockSpec(memory_space=pltpu.VMEM)
    hbm = pl.BlockSpec(memory_space=pltpu.HBM)
    dma = pltpu.SemaphoreType.DMA

    def fixed(x):
        return pltpu.with_memory_space_constraint(x, pltpu.HBM)

    return pl.pallas_call(
        functools.partial(fused_kernel, n_space, n_chan, bricks, slots),
        out_shape=jax.ShapeDtypeStruct((own, slots * cells), BF),
        in_specs=[hbm] * 10,
        out_specs=vmem,
        scratch_shapes=[
            pltpu.VMEM(features.shape, BF),
            pltpu.VMEM(neighbours.shape, jnp.int32),
            pltpu.VMEM(conv_fine.shape, BF),
            pltpu.VMEM((group, TAPS2 * PAD * fine), BF),
            pltpu.VMEM((1, own), F32),
            pltpu.VMEM((1, bricks), jnp.int32),
            pltpu.VMEM((1, bricks), jnp.int32),
            pltpu.VMEM((1, parents), jnp.int32),
            pltpu.VMEM((8, 128), jnp.int32),
            pltpu.VMEM(conv_down.shape, BF),
            pltpu.VMEM(conv_coarse.shape, BF),
            pltpu.VMEM((n_chan * group, n_chan * group), BF),
            pltpu.VMEM((2, bricks, FACE, fine), BF),
            pltpu.VMEM((2, 8, 128), jnp.int32),
            pltpu.VMEM((PAD, PAD, bricks, PAD * fine), BF),
            pltpu.VMEM((2, EDGE * bricks, group), F32),
            pltpu.VMEM((n_chan, LOW, EDGE * bricks, group), BF),
            pltpu.VMEM((LOW, LOW, bricks, LOW * fine), BF),
            pltpu.VMEM((n_chan, HALF * HALF * bricks, HALF * own_d), BF),
            pltpu.VMEM((n_chan, HALF * bricks, HALF * own_d), BF),
            pltpu.VMEM((n_chan, HALF * bricks, HALF * own_d), BF),
            pltpu.VMEM((CX + 2, TAPS2 * CLAYER, coarse), BF),
            pltpu.VMEM((CX, TAPS2 * CLAYER, HALF**3 * bricks), BF),
            pltpu.VMEM((2, TAPS2 * CLAYER, HALF**2 * bricks), BF),
            pltpu.VMEM((own, parents * cells), F32),
            pltpu.VMEM((3, own, parents * cells), BF),
            pltpu.VMEM((3, n_chan, 1, parents * cells), F32),
            pltpu.VMEM((3, slots * cells, parents * cells), BF),
            dma((10,)),
            dma((2, 2)),
            dma((2, 2)),
            dma((3, n_chan - 1)),
            dma((3, n_chan)),
            dma((n_chan,)),
            dma((n_chan,)),
            dma((HALF, n_chan - 1)),
            dma((HALF, n_chan)),
            dma((2, n_chan)),
            dma((2, n_chan)),
            dma((2,)),
            dma((2,)),
            dma((3, n_chan)),
            dma((3, n_chan)),
        ],
        compiler_params=pltpu.CompilerParams(
            collective_id=0, has_side_effects=True, vmem_limit_bytes=40000000
        ),
    )(
        fixed(features),
        fixed(neighbours),
        fixed(parent_index.reshape(1, -1)),
        fixed(octant.reshape(1, -1)),
        fixed(parent_dest.reshape(1, -1)),
        fixed(conv_fine),
        fixed(conv_down),
        fixed(conv_coarse),
        fixed(norm_gain.reshape(1, -1)),
        fixed(table(n_chan, fine)),
    )


def solution(mesh):
    sizes = dict(mesh.shape)
    return jax.shard_map(
        functools.partial(body, sizes["space"], sizes["chan"]),
        mesh=mesh,
        in_specs=(
            P("space", None, None),
            P("space", None),
            P("space"),
            P("space"),
            P("space"),
            P("chan", None),
            P("chan", None),
            P("chan", None),
            P("chan"),
        ),
        out_specs=P("chan", "space"),
        check_vma=False,
    )
```

```python
import functools

import jax
import jax.numpy as jnp
import numpy as np
from jax import lax
from jax.experimental import pallas as pl
from jax.experimental.pallas import tpu as pltpu
from jax.sharding import PartitionSpec as P

EDGE = 4
SLAB_Y = 4
SLAB_Z = 4
PAD = EDGE + 2
LOW = EDGE + 1
HALF = EDGE // 2
FACE = EDGE * EDGE
CY = SLAB_Y * HALF
CZ = SLAB_Z * HALF
CLAYER = CY * CZ
CX = 2 * HALF
TAPS2 = 9
epsilon = 1e-06
FAR = 1 << 20
BF = jnp.bfloat16
F32 = jnp.float32
NT = (((1,), (1,)), ((), ()))


def iota(shape, dim):
    return lax.broadcasted_iota(jnp.int32, shape, dim)


def one(cond):
    return jnp.where(cond, 1.0, 0.0).astype(BF)


def pick(a, b):
    return jnp.dot(a, b, preferred_element_type=F32)


def tap2(b, c):
    return 3 * (b + 1) + c + 1


def source(pos):
    if pos == 0:
        return -1, EDGE - 1
    if pos == EDGE + 1:
        return 1, 0
    return 0, pos - 1


def table(n_chan, fine):
    wide = fine // n_chan
    r = np.arange(n_chan * EDGE * wide)[:, None]
    q = np.arange(n_chan * EDGE * wide)[None, :]
    group = EDGE * wide
    perm = (r % group) // wide * fine + r // group * wide + r % wide == q
    return jnp.asarray(np.asarray(perm, np.float32).astype(jnp.bfloat16))


def fused_kernel(
    n_space, n_chan, bricks, slots,
    feat_hbm, nbr_hbm, parent_hbm, octant_hbm, dest_hbm, wf_hbm, wd_hbm, wc_hbm, gain_hbm, perm_hbm,
    out,
    feat, nbr, wf, wt, gain, parent_in, octant_in, dest_in, meta, wd, wc, perm,
    fh, mh, pbuf, part_h, g_buf, qbuf, c_buf, cp, cn, e_buf, hot_e, acc, pair, single, kept, pb, pw, ohd,
    wsem, s1, r1, s2, r2, hs2, hr2, s3, r3, hs3, hr3, s4, r4, ws4, wr4,
):
    sp = lax.axis_index("space")
    me = lax.axis_index("chan")
    has_prev = sp > 0
    has_next = sp < n_space - 1
    fine = feat.shape[2]
    wide = fine // n_chan
    parents = dest_in.shape[1]
    cells = EDGE**3
    own_d = wd.shape[0]
    coarse = own_d * n_chan
    group = EDGE * wide
    line = EDGE * bricks
    side = HALF * bricks

    def rc(src, dst, ss, rs, space, chan):
        return pltpu.make_async_remote_copy(
            src_ref=src,
            dst_ref=dst,
            send_sem=ss,
            recv_sem=rs,
            device_id={"space": space, "chan": chan},
            device_id_type=pl.DeviceIdType.MESH,
        )

    peers = [lax.rem(me + k, n_chan) for k in range(1, n_chan)]
    barrier = pltpu.get_barrier_semaphore()

    def greet(space, chan):
        pl.semaphore_signal(
            barrier,
            inc=1,
            device_id={"space": space, "chan": chan},
            device_id_type=pl.DeviceIdType.MESH,
        )

    @pl.when(has_prev)
    def _():
        greet(sp - 1, me)

    @pl.when(has_next)
    def _():
        greet(sp + 1, me)

    for chan in peers:
        greet(sp, chan)

    loads = [
        pltpu.make_async_copy(src, dst, wsem.at[k])
        for k, (src, dst) in enumerate(
            (
                (nbr_hbm, nbr),
                (feat_hbm, feat),
                (parent_hbm, parent_in),
                (octant_hbm, octant_in),
                (dest_hbm, dest_in),
                (wf_hbm, wf),
                (perm_hbm, perm),
                (wd_hbm, wd),
                (gain_hbm, gain),
                (wc_hbm, wc),
            )
        )
    ]
    for load in loads:
        load.start()

    up_feat = rc(feat_hbm.at[:, pl.ds((EDGE - 1) * FACE, FACE), :], fh.at[0], s1.at[0, 0], r1.at[0, 0], sp + 1, me)
    up_meta = rc(meta, mh.at[0], s1.at[0, 1], r1.at[0, 1], sp + 1, me)
    dn_feat = rc(feat_hbm.at[:, pl.ds(0, FACE), :], fh.at[1], s1.at[1, 0], r1.at[1, 0], sp - 1, me)
    dn_meta = rc(meta, mh.at[1], s1.at[1, 1], r1.at[1, 1], sp - 1, me)

    pl.semaphore_wait(barrier, n_chan - 1 + has_prev.astype(jnp.int32) + has_next.astype(jnp.int32))

    @pl.when(has_next)
    def _():
        up_feat.start()

    @pl.when(has_prev)
    def _():
        dn_feat.start()

    @pl.when(jnp.logical_not(has_prev))
    def _():
        fh[0] = jnp.zeros(fh.shape[1:], BF)
        mh[0] = jnp.zeros(mh.shape[1:], jnp.int32)
        for s in range(n_chan):
            g_buf[s, 0] = jnp.zeros(g_buf.shape[2:], BF)
        cp[...] = jnp.zeros(cp.shape, BF)
        pb[0] = jnp.zeros(pb.shape[1:], BF)
        pw[0] = jnp.zeros(pw.shape[1:], F32)

    @pl.when(jnp.logical_not(has_next))
    def _():
        fh[1] = jnp.zeros(fh.shape[1:], BF)
        mh[1] = jnp.zeros(mh.shape[1:], jnp.int32)
        cn[...] = jnp.zeros(cn.shape, BF)
        pb[2] = jnp.zeros(pb.shape[1:], BF)
        pw[2] = jnp.zeros(pw.shape[1:], F32)

    reach = PAD * fine
    for z in range(EDGE):
        for bc in range(TAPS2):
            at = bc * reach
            rows = slice(z * wide, (z + 1) * wide)
            if z > 0:
                wt[rows, at : at + z * fine] = jnp.zeros((wide, z * fine), BF)
            if z < EDGE - 1:
                wt[rows, at + (z + 3) * fine : at + reach] = jnp.zeros((wide, (EDGE - 1 - z) * fine), BF)
    meta[...] = jnp.zeros(meta.shape, jnp.int32)

    for load in loads[2:5]:
        load.wait()
    local = parent_in[...] - sp * parents
    octant = octant_in[...]
    y_pos = 2 * (local // (SLAB_Z // 2)) + octant // 2 % 2
    z_pos = 2 * (local % (SLAB_Z // 2)) + octant // 4
    meta[0:1, 0:bricks] = octant % 2 + 2 * y_pos + 2 * SLAB_Y * z_pos
    meta[1:2, 0:parents] = dest_in[...] - (sp - 1) * slots

    @pl.when(has_next)
    def _():
        up_meta.start()

    @pl.when(has_prev)
    def _():
        dn_meta.start()

    for load in loads[0:2]:
        load.wait()
    raw = nbr[...]
    loc = jnp.where(raw >= 0, raw - bricks * (sp - 1), -FAR)
    here = iota((bricks, 1), 0) + bricks

    def loc_of(a, b, c):
        k = 9 * (a + 1) + tap2(b, c)
        if k == 13:
            return here
        k = k - (k > 13)
        return loc[:, k : k + 1]

    def place(a, first, sources, planes):
        wide_k = sources.shape[0]
        col = iota((bricks, wide_k), 1)
        keys = {
            (b, c): jnp.broadcast_to((loc_of(a, b, c) - first) * FACE, (bricks, wide_k))
            for b in (-1, 0, 1)
            for c in (-1, 0, 1)
        }
        for zq in range(PAD):
            c, sz = source(zq)
            hots = []
            for yq in range(PAD):
                b, sy = source(yq)
                hots.append(one(col == keys[b, c] + (sy * EDGE + sz)))
            placed = pick(jnp.concatenate(hots, axis=0), sources).astype(BF)
            for i, xq in enumerate(planes):
                pbuf[xq, :, :, zq * fine : (zq + 1) * fine] = placed[:, i * fine : (i + 1) * fine].reshape(
                    PAD, bricks, fine
                )

    def plane(i):
        return feat[:, i * FACE : (i + 1) * FACE, :].reshape(bricks * FACE, fine)

    place(0, bricks, jnp.concatenate([plane(i) for i in range(EDGE)], axis=1), range(1, EDGE + 1))
    place(-1, bricks, plane(EDGE - 1), [0])
    place(1, bricks, plane(0), [EDGE + 1])

    loads[5].wait()
    for z in range(EDGE):
        for bc in range(TAPS2):
            at = bc * reach + z * fine
            wt[z * wide : (z + 1) * wide, at : at + 3 * fine] = wf[:, bc * 3 * fine : (bc + 1) * 3 * fine]

    def cube(x, b):
        return pbuf[x, b : b + EDGE].reshape(line, reach)

    parts = []
    for a in range(3):
        for b in range(3):
            parts.append(jnp.concatenate([cube(x + a, b) for x in range(EDGE)], axis=0))
    total = lax.dot_general(jnp.concatenate(parts, axis=1), wt[...], NT, preferred_element_type=F32)
    part_h[0] = total[0:line]
    part_h[1] = total[(EDGE - 1) * line :]
    for x in range(1, EDGE - 1):
        g_buf[me, x + 1] = jnp.maximum(total[x * line : (x + 1) * line], 0.0).astype(BF)

    def rest(a, xq):
        taps = wt[:, (a + 1) * 3 * reach : (a + 2) * 3 * reach]
        return lax.dot_general(
            jnp.concatenate([cube(xq, b) for b in range(3)], axis=1), taps, NT, preferred_element_type=F32
        )

    spans = ((2, EDGE - 2), (EDGE, 1), (1, 1))

    def hid_copy(j, k, chan):
        ref = g_buf.at[me, pl.ds(*spans[j])]
        return rc(ref, ref, s2.at[j, k], r2.at[j, me], sp, chan)

    def hid_wait(j):
        for k in range(1, n_chan):
            src = lax.rem(me + k, n_chan)
            ref = g_buf.at[src, pl.ds(*spans[j])]
            rc(ref, ref, s2.at[j, 0], r2.at[j, src], sp, src).wait_recv()

    for k, chan in enumerate(peers):
        hid_copy(0, k, chan).start()

    @pl.when(has_next)
    def _():
        dn_feat.wait_recv()

    @pl.when(has_prev)
    def _():
        up_feat.wait_recv()

    place(1, 2 * bricks, fh[1].reshape(bricks * FACE, fine), [EDGE + 1])
    g_buf[me, EDGE] = jnp.maximum(part_h[1] + rest(1, EDGE + 1), 0.0).astype(BF)
    for k, chan in enumerate(peers):
        hid_copy(1, k, chan).start()

    place(-1, 0, fh[0].reshape(bricks * FACE, fine), [0])
    g_buf[me, 1] = jnp.maximum(part_h[0] + rest(-1, 0), 0.0).astype(BF)
    for k, chan in enumerate(peers):
        hid_copy(2, k, chan).start()

    twin = me + 1 - 2 * lax.rem(me, 2)
    spread_to = [lax.rem(c + 2 * j, n_chan) for j in range(n_chan // 2) for c in (me, twin)]

    def hid_halo(k):
        return rc(g_buf.at[me, EDGE], g_buf.at[me, 0], hs2.at[k], hr2.at[me], sp + 1, spread_to[k])

    @pl.when(has_next)
    def _():
        for k in range(n_chan):
            hid_halo(k).start()

    @pl.when(has_next)
    def _():
        dn_meta.wait_recv()

    @pl.when(has_prev)
    def _():
        up_meta.wait_recv()

    lanes = meta.shape[1]
    lane_par = jnp.where(
        iota((lanes, parents * cells), 1) % CLAYER // FACE == iota((lanes, parents * cells), 0), 1.0, 0.0
    )

    def dest_table(k):
        block = meta[...] if k == 1 else mh[k // 2]
        rel = jnp.dot(block.astype(F32), lane_par, preferred_element_type=F32)[1:2].astype(jnp.int32)
        slot = rel - (2 - k) * slots
        at = iota((1, parents * cells), 1)
        row = at % (HALF * CLAYER)
        target = slot * cells + (2 * (row // CLAYER) + at // (HALF * CLAYER)) * FACE + at % FACE
        ids = iota((slots * cells, parents * cells), 0)
        ohd[k] = one(ids == jnp.where((slot >= 0) & (slot < slots), target, -1))

    n_hot = HALF * HALF * bricks
    spread = jnp.where(iota((lanes, n_hot), 1) % bricks == iota((lanes, n_hot), 0), 1.0, 0.0)

    def key_of(block):
        code = jnp.dot(block.astype(F32), spread, preferred_element_type=F32)[0:1].astype(jnp.int32)
        sub = iota((1, n_hot), 1) // bricks
        y = 2 * (code // 2 % SLAB_Y) + sub % HALF
        z = 2 * (code // (2 * SLAB_Y)) + sub // HALF
        return code % 2, y * CZ + z

    keys = [(mh[0], 1), (meta[...], 0), (meta[...], 1), (mh[1], 0)]
    keys = [jnp.where(x_bit == want, key, -1) for (x_bit, key), want in ((key_of(m), w) for m, w in keys)]
    at = iota((CLAYER, n_hot), 0)
    par, yz = at // FACE, at % FACE
    for bc in range(TAPS2):
        y = par // (SLAB_Z // 2) * EDGE + yz // EDGE + bc // 3 - 1
        z = par % (SLAB_Z // 2) * EDGE + yz % EDGE + bc % 3 - 1
        want = jnp.where((y >= 0) & (y < CY) & (z >= 0) & (z < CZ), y * CZ + z, FAR)
        for k in range(4):
            hot_e[k, bc * CLAYER : (bc + 1) * CLAYER] = one(want == keys[k])

    for k in range(3):
        dest_table(k)

    for load in loads[6:8]:
        load.wait()

    hid_wait(0)

    full = EDGE * fine
    tail = fine * (EDGE - 1)

    def unpack(at):
        joined = jnp.concatenate(
            [jnp.concatenate([g_buf[s, x + 1] for s in range(n_chan)], axis=1) for x in at], axis=0
        )
        moved = pick(joined, perm[...]).astype(BF)
        return [moved[i * line : (i + 1) * line] for i in range(len(at))]

    def hot_rows(a, c, n):
        col = iota((bricks, n), 1)
        rows = []
        for yq in range(LOW):
            b, sy = source(yq)
            where = loc_of(a, b, c)
            where = jnp.where(where >= bricks, where - bricks, where + line) + sy * bricks
            rows.append(one(col == where))
        return jnp.concatenate(rows, axis=0)

    def lay_out(at):
        moved = unpack(at)
        edge_y = pick(
            one(iota((bricks, bricks), 1) == loc_of(0, -1, 0) - bricks),
            jnp.concatenate([m[line - bricks :] for m in moved], axis=1),
        ).astype(BF)
        edge_z = pick(hot_rows(0, -1, line), jnp.concatenate([m[:, tail:] for m in moved], axis=1)).astype(BF)
        for i, x in enumerate(at):
            qbuf[x + 1, 1:LOW, :, fine : LOW * fine] = moved[i].reshape(EDGE, bricks, full)
            qbuf[x + 1, 0, :, fine : LOW * fine] = edge_y[:, i * full : (i + 1) * full]
            qbuf[x + 1, :, :, 0:fine] = edge_z[:, i * fine : (i + 1) * fine].reshape(LOW, bricks, fine)
        return moved

    lay_out(list(range(1, EDGE - 1)))

    for j in (1, 2):
        hid_wait(j)

    def down(qx):
        stacked = []
        for qz in range(HALF):
            for qy in range(HALF):
                stacked.append(
                    jnp.concatenate(
                        [
                            qbuf[2 * qx + a, 2 * qy + b, :, 2 * qz * fine : (2 * qz + 3) * fine]
                            for a in range(3)
                            for b in range(3)
                        ],
                        axis=1,
                    )
                )
        pieces = lax.dot_general(jnp.concatenate(stacked, axis=0), wd[...], NT, preferred_element_type=F32)
        pieces = jnp.maximum(pieces, 0.0)
        c_buf[me, qx * side : (qx + 1) * side] = jnp.concatenate(
            [pieces[h * side : (h + 1) * side] for h in range(HALF)], axis=1
        ).astype(BF)

    def part_copy(qx, k, chan):
        ref = c_buf.at[me, pl.ds(qx * side, side)]
        return rc(ref, ref, s3.at[qx, k], r3.at[qx, me], sp, chan)

    def up_part(k):
        return rc(c_buf.at[me, pl.ds(side, side)], cp.at[me], hs3.at[0, k], hr3.at[0, me], sp + 1, spread_to[k])

    def dn_part(k):
        return rc(c_buf.at[me, pl.ds(0, side)], cn.at[me], hs3.at[1, k], hr3.at[1, me], sp - 1, spread_to[k])

    last = lay_out([0, EDGE - 1])[1]
    down(1)
    for k, chan in enumerate(peers):
        part_copy(1, k, chan).start()

    @pl.when(has_next)
    def _():
        for k in range(n_chan):
            up_part(k).start()

    @pl.when(has_prev)
    def _():
        for chan in range(n_chan):
            rc(g_buf.at[chan, 0], g_buf.at[chan, 0], hs2.at[chan], hr2.at[chan], sp - 1, chan).wait_recv()

    joint = jnp.concatenate(
        [last, pick(jnp.concatenate([g_buf[s, 0] for s in range(n_chan)], axis=1), perm[...]).astype(BF)], axis=0
    )
    qbuf[0, :, :, fine : LOW * fine] = pick(hot_rows(-1, 0, 2 * line), joint).astype(BF).reshape(LOW, bricks, full)
    qbuf[0, :, :, 0:fine] = pick(hot_rows(-1, -1, 2 * line), joint[:, tail:]).astype(BF).reshape(LOW, bricks, fine)
    down(0)

    for k, chan in enumerate(peers):
        part_copy(0, k, chan).start()

    @pl.when(has_prev)
    def _():
        for k in range(n_chan):
            dn_part(k).start()

    for load in loads[8:]:
        load.wait()
    own = gain.shape[1]
    gain_col = jnp.sum(
        jnp.where(iota((own, own), 0) == iota((own, own), 1), gain[...], 0.0), axis=1, keepdims=True
    )

    def part_wait(qx):
        for k in range(1, n_chan):
            src = lax.rem(me + k, n_chan)
            ref = c_buf.at[src, pl.ds(qx * side, side)]
            rc(ref, ref, s3.at[qx, 0], r3.at[qx, src], sp, src).wait_recv()

    def all_channels(blocks):
        return jnp.concatenate(
            [
                jnp.concatenate([block[:, h * own_d : (h + 1) * own_d] for block in blocks], axis=1)
                for h in range(HALF)
            ],
            axis=0,
        )

    def fill(qx):
        inside = all_channels([c_buf[s, qx * side : (qx + 1) * side] for s in range(n_chan)])
        for x_bit in range(2):
            e_buf[2 * x_bit + qx + 1] = pick(hot_e[1 + x_bit], inside).astype(BF)

    span = TAPS2 * coarse

    def blocks(layers):
        return [
            jnp.concatenate([e_buf[x, bc * CLAYER : (bc + 1) * CLAYER] for x in layers], axis=0)
            for bc in range(TAPS2)
        ]

    def tap(a, layers):
        return lax.dot_general(
            wc[:, a * span : (a + 1) * span], jnp.concatenate(blocks(layers), axis=1), NT, preferred_element_type=F32
        )

    def pb_copy(side_k, h):
        step = 1 - 2 * side_k
        return rc(pb.at[1, h], pb.at[2 * side_k, h], s4.at[side_k, h], r4.at[side_k, h], sp + step, me)

    def settle(h, total):
        rounded = total.astype(BF)
        pb[1, h] = rounded
        values = rounded.astype(F32)
        pw[1, me, h] = jnp.sum(values * values, axis=0, keepdims=True)

        @pl.when(has_next)
        def _():
            pb_copy(0, h).start()

        @pl.when(has_prev)
        def _():
            pb_copy(1, h).start()

    part_wait(1)
    fill(1)
    acc[1] = tap(1, [2, 4])
    pair[0] = tap(2, [2, 4])
    single[0] = tap(0, [2])
    @pl.when(has_prev)
    def _():
        for chan in range(n_chan):
            rc(cp.at[chan], cp.at[chan], hs3.at[0, chan], hr3.at[0, chan], sp - 1, chan).wait_recv()

    e_buf[0] = pick(hot_e[0], all_channels([cp[s] for s in range(n_chan)])).astype(BF)
    acc[0] = pair[0] + jnp.concatenate([tap(0, [0]), single[0]], axis=1)
    part_wait(0)
    fill(0)
    acc[0] += tap(1, [1, 3])
    pair[1] = acc[1] + tap(0, [1, 3])
    single[1] = tap(2, [3])
    settle(0, acc[0])
    @pl.when(has_next)
    def _():
        for chan in range(n_chan):
            rc(cn.at[chan], cn.at[chan], hs3.at[1, chan], hr3.at[1, chan], sp + 1, chan).wait_recv()

    e_buf[CX + 1] = pick(hot_e[3], all_channels([cn[s] for s in range(n_chan)])).astype(BF)
    settle(1, pair[1] + jnp.concatenate([single[1], tap(2, [5])], axis=1))

    for k, chan in enumerate(peers):
        rc(pw.at[1, me], pw.at[1, me], ws4.at[1, k], wr4.at[1, me], sp, chan).start()

    @pl.when(has_next)
    def _():
        for k in range(n_chan):
            rc(pw.at[1, me], pw.at[0, me], ws4.at[0, k], wr4.at[0, me], sp + 1, spread_to[k]).start()

    @pl.when(has_prev)
    def _():
        for k in range(n_chan):
            rc(pw.at[1, me], pw.at[2, me], ws4.at[2, k], wr4.at[2, me], sp - 1, spread_to[k]).start()

    def normed(k):
        halves = []
        for h in range(HALF):
            power = pw[k, 0, h]
            for s in range(1, n_chan):
                power = power + pw[k, s, h]
            halves.append((pb[k, h].astype(F32) * lax.rsqrt(power / coarse + epsilon) * gain_col).astype(BF))
        return lax.dot_general(jnp.concatenate(halves, axis=1), ohd[k], NT, preferred_element_type=F32)

    for k in range(1, n_chan):
        src = lax.rem(me + k, n_chan)
        rc(pw.at[1, src], pw.at[1, src], ws4.at[1, 0], wr4.at[1, src], sp, src).wait_recv()
    kept[...] = normed(1)

    @pl.when(has_prev)
    def _():
        for h in range(HALF):
            pb_copy(0, h).wait_recv()
        for chan in range(n_chan):
            rc(pw.at[0, chan], pw.at[0, chan], ws4.at[0, chan], wr4.at[0, chan], sp - 1, chan).wait_recv()

    @pl.when(has_next)
    def _():
        for h in range(HALF):
            pb_copy(1, h).wait_recv()
        for chan in range(n_chan):
            rc(pw.at[2, chan], pw.at[2, chan], ws4.at[2, chan], wr4.at[2, chan], sp + 1, chan).wait_recv()

    out[...] = (kept[...] + normed(0) + normed(2)).astype(BF)

    for k, chan in enumerate(peers):
        for j in range(3):
            hid_copy(j, k, chan).wait_send()
        for qx in range(HALF):
            part_copy(qx, k, chan).wait_send()
        rc(pw.at[1, me], pw.at[1, me], ws4.at[1, k], wr4.at[1, me], sp, chan).wait_send()

    @pl.when(has_next)
    def _():
        up_meta.wait_send()
        up_feat.wait_send()
        for h in range(HALF):
            pb_copy(0, h).wait_send()
        for chan in range(n_chan):
            hid_halo(chan).wait_send()
            up_part(chan).wait_send()
            rc(pw.at[1, me], pw.at[0, me], ws4.at[0, chan], wr4.at[0, me], sp + 1, spread_to[chan]).wait_send()

    @pl.when(has_prev)
    def _():
        dn_meta.wait_send()
        dn_feat.wait_send()
        for h in range(HALF):
            pb_copy(1, h).wait_send()
        for chan in range(n_chan):
            dn_part(chan).wait_send()
            rc(pw.at[1, me], pw.at[2, me], ws4.at[2, chan], wr4.at[2, me], sp - 1, spread_to[chan]).wait_send()


def body(n_space, n_chan, features, neighbours, parent_index, octant, parent_dest, conv_fine, conv_down, conv_coarse, norm_gain):
    bricks, _, fine = features.shape
    parents = parent_dest.shape[0]
    slots = 2 * parents
    own_d = conv_down.shape[0]
    own = conv_coarse.shape[0]
    cells = EDGE**3
    coarse = own_d * n_chan
    group = EDGE * fine // n_chan
    vmem = pl.BlockSpec(memory_space=pltpu.VMEM)
    hbm = pl.BlockSpec(memory_space=pltpu.HBM)
    dma = pltpu.SemaphoreType.DMA

    def fixed(x):
        return pltpu.with_memory_space_constraint(x, pltpu.HBM)

    return pl.pallas_call(
        functools.partial(fused_kernel, n_space, n_chan, bricks, slots),
        out_shape=jax.ShapeDtypeStruct((own, slots * cells), BF),
        in_specs=[hbm] * 10,
        out_specs=vmem,
        scratch_shapes=[
            pltpu.VMEM(features.shape, BF),
            pltpu.VMEM(neighbours.shape, jnp.int32),
            pltpu.VMEM(conv_fine.shape, BF),
            pltpu.VMEM((group, TAPS2 * PAD * fine), BF),
            pltpu.VMEM((1, own), F32),
            pltpu.VMEM((1, bricks), jnp.int32),
            pltpu.VMEM((1, bricks), jnp.int32),
            pltpu.VMEM((1, parents), jnp.int32),
            pltpu.VMEM((8, 128), jnp.int32),
            pltpu.VMEM(conv_down.shape, BF),
            pltpu.VMEM(conv_coarse.shape, BF),
            pltpu.VMEM((n_chan * group, n_chan * group), BF),
            pltpu.VMEM((2, bricks, FACE, fine), BF),
            pltpu.VMEM((2, 8, 128), jnp.int32),
            pltpu.VMEM((PAD, PAD, bricks, PAD * fine), BF),
            pltpu.VMEM((2, EDGE * bricks, group), F32),
            pltpu.VMEM((n_chan, LOW, EDGE * bricks, group), BF),
            pltpu.VMEM((LOW, LOW, bricks, LOW * fine), BF),
            pltpu.VMEM((n_chan, HALF * HALF * bricks, HALF * own_d), BF),
            pltpu.VMEM((n_chan, HALF * bricks, HALF * own_d), BF),
            pltpu.VMEM((n_chan, HALF * bricks, HALF * own_d), BF),
            pltpu.VMEM((CX + 2, TAPS2 * CLAYER, coarse), BF),
            pltpu.VMEM((4, TAPS2 * CLAYER, HALF**2 * bricks), BF),
            pltpu.VMEM((HALF, own, HALF * CLAYER), F32),
            pltpu.VMEM((HALF, own, HALF * CLAYER), F32),
            pltpu.VMEM((HALF, own, CLAYER), F32),
            pltpu.VMEM((own, slots * cells), F32),
            pltpu.VMEM((3, HALF, own, HALF * CLAYER), BF),
            pltpu.VMEM((3, n_chan, HALF, 1, HALF * CLAYER), F32),
            pltpu.VMEM((3, slots * cells, parents * cells), BF),
            dma((10,)),
            dma((2, 2)),
            dma((2, 2)),
            dma((3, n_chan - 1)),
            dma((3, n_chan)),
            dma((n_chan,)),
            dma((n_chan,)),
            dma((HALF, n_chan - 1)),
            dma((HALF, n_chan)),
            dma((2, n_chan)),
            dma((2, n_chan)),
            dma((2, HALF)),
            dma((2, HALF)),
            dma((3, n_chan)),
            dma((3, n_chan)),
        ],
        compiler_params=pltpu.CompilerParams(
            collective_id=0, has_side_effects=True, vmem_limit_bytes=40000000
        ),
    )(
        fixed(features),
        fixed(neighbours),
        fixed(parent_index.reshape(1, -1)),
        fixed(octant.reshape(1, -1)),
        fixed(parent_dest.reshape(1, -1)),
        fixed(conv_fine),
        fixed(conv_down),
        fixed(conv_coarse),
        fixed(norm_gain.reshape(1, -1)),
        fixed(table(n_chan, fine)),
    )


def solution(mesh):
    sizes = dict(mesh.shape)
    return jax.shard_map(
        functools.partial(body, sizes["space"], sizes["chan"]),
        mesh=mesh,
        in_specs=(
            P("space", None, None),
            P("space", None),
            P("space"),
            P("space"),
            P("space"),
            P("chan", None),
            P("chan", None),
            P("chan", None),
            P("chan"),
        ),
        out_specs=P("chan", "space"),
        check_vma=False,
    )
```

```python
import functools

import jax
import jax.numpy as jnp
import numpy as np
from jax import lax
from jax.experimental import pallas as pl
from jax.experimental.pallas import tpu as pltpu
from jax.sharding import PartitionSpec as P

EDGE = 4
SLAB_Y = 4
SLAB_Z = 4
PAD = EDGE + 2
LOW = EDGE + 1
HALF = EDGE // 2
FACE = EDGE * EDGE
CY = SLAB_Y * HALF
CZ = SLAB_Z * HALF
CLAYER = CY * CZ
CX = 2 * HALF
TAPS2 = 9
epsilon = 1e-06
FAR = 1 << 20
BF = jnp.bfloat16
F32 = jnp.float32
NT = (((1,), (1,)), ((), ()))


def iota(shape, dim):
    return lax.broadcasted_iota(jnp.int32, shape, dim)


def one(cond):
    return jnp.where(cond, 1.0, 0.0).astype(BF)


def pick(a, b):
    return jnp.dot(a, b, preferred_element_type=F32)


def tap2(b, c):
    return 3 * (b + 1) + c + 1


def source(pos):
    if pos == 0:
        return -1, EDGE - 1
    if pos == EDGE + 1:
        return 1, 0
    return 0, pos - 1


def table(n_chan, fine):
    wide = fine // n_chan
    r = np.arange(n_chan * EDGE * wide)[:, None]
    q = np.arange(n_chan * EDGE * wide)[None, :]
    group = EDGE * wide
    perm = (r % group) // wide * fine + r // group * wide + r % wide == q
    return jnp.asarray(np.asarray(perm, np.float32).astype(jnp.bfloat16))


def fused_kernel(
    n_space, n_chan, bricks, slots,
    feat_hbm, nbr_hbm, parent_hbm, octant_hbm, dest_hbm, wf_hbm, wd_hbm, wc_hbm, gain_hbm, perm_hbm,
    out,
    feat, nbr, wf, wt, gain, parent_in, octant_in, dest_in, meta, wd, wc, perm,
    fh, mh, pbuf, part_h, g_buf, qbuf, c_buf, cp, cn, e_buf, hot_e, acc, pair, single, kept, kept_row, base, pb, pw, ohd,
    wsem, s1, r1, s2, r2, hs2, hr2, s3, r3, hs3, hr3, s4, r4, ws4, wr4,
):
    sp = lax.axis_index("space")
    me = lax.axis_index("chan")
    has_prev = sp > 0
    has_next = sp < n_space - 1
    fine = feat.shape[2]
    wide = fine // n_chan
    parents = dest_in.shape[1]
    cells = EDGE**3
    own_d = wd.shape[0]
    coarse = own_d * n_chan
    group = EDGE * wide
    line = EDGE * bricks
    side = HALF * bricks

    def rc(src, dst, ss, rs, space, chan):
        return pltpu.make_async_remote_copy(
            src_ref=src,
            dst_ref=dst,
            send_sem=ss,
            recv_sem=rs,
            device_id={"space": space, "chan": chan},
            device_id_type=pl.DeviceIdType.MESH,
        )

    peers = [lax.rem(me + k, n_chan) for k in range(1, n_chan)]
    barrier = pltpu.get_barrier_semaphore()

    def greet(space, chan):
        pl.semaphore_signal(
            barrier,
            inc=1,
            device_id={"space": space, "chan": chan},
            device_id_type=pl.DeviceIdType.MESH,
        )

    @pl.when(has_prev)
    def _():
        greet(sp - 1, me)

    @pl.when(has_next)
    def _():
        greet(sp + 1, me)

    for chan in peers:
        greet(sp, chan)

    loads = [
        pltpu.make_async_copy(src, dst, wsem.at[k])
        for k, (src, dst) in enumerate(
            (
                (nbr_hbm, nbr),
                (feat_hbm, feat),
                (parent_hbm, parent_in),
                (octant_hbm, octant_in),
                (dest_hbm, dest_in),
                (wf_hbm, wf),
                (perm_hbm, perm),
                (wd_hbm, wd),
                (gain_hbm, gain),
                (wc_hbm, wc),
            )
        )
    ]
    for load in loads:
        load.start()

    up_feat = rc(feat_hbm.at[:, pl.ds((EDGE - 1) * FACE, FACE), :], fh.at[0], s1.at[0, 0], r1.at[0, 0], sp + 1, me)
    up_meta = rc(meta, mh.at[0], s1.at[0, 1], r1.at[0, 1], sp + 1, me)
    dn_feat = rc(feat_hbm.at[:, pl.ds(0, FACE), :], fh.at[1], s1.at[1, 0], r1.at[1, 0], sp - 1, me)
    dn_meta = rc(meta, mh.at[1], s1.at[1, 1], r1.at[1, 1], sp - 1, me)

    pl.semaphore_wait(barrier, n_chan - 1 + has_prev.astype(jnp.int32) + has_next.astype(jnp.int32))

    @pl.when(has_next)
    def _():
        up_feat.start()

    @pl.when(has_prev)
    def _():
        dn_feat.start()

    @pl.when(jnp.logical_not(has_prev))
    def _():
        fh[0] = jnp.zeros(fh.shape[1:], BF)
        mh[0] = jnp.zeros(mh.shape[1:], jnp.int32)
        for s in range(n_chan):
            g_buf[s, 0] = jnp.zeros(g_buf.shape[2:], BF)
        cp[...] = jnp.zeros(cp.shape, BF)
        pb[0] = jnp.zeros(pb.shape[1:], BF)
        pw[0] = jnp.zeros(pw.shape[1:], F32)

    @pl.when(jnp.logical_not(has_next))
    def _():
        fh[1] = jnp.zeros(fh.shape[1:], BF)
        mh[1] = jnp.zeros(mh.shape[1:], jnp.int32)
        cn[...] = jnp.zeros(cn.shape, BF)
        pb[2] = jnp.zeros(pb.shape[1:], BF)
        pw[2] = jnp.zeros(pw.shape[1:], F32)

    reach = PAD * fine
    for z in range(EDGE):
        for bc in range(TAPS2):
            at = bc * reach
            rows = slice(z * wide, (z + 1) * wide)
            if z > 0:
                wt[rows, at : at + z * fine] = jnp.zeros((wide, z * fine), BF)
            if z < EDGE - 1:
                wt[rows, at + (z + 3) * fine : at + reach] = jnp.zeros((wide, (EDGE - 1 - z) * fine), BF)
    meta[...] = jnp.zeros(meta.shape, jnp.int32)

    for load in loads[2:5]:
        load.wait()
    local = parent_in[...] - sp * parents
    octant = octant_in[...]
    y_pos = 2 * (local // (SLAB_Z // 2)) + octant // 2 % 2
    z_pos = 2 * (local % (SLAB_Z // 2)) + octant // 4
    meta[0:1, 0:bricks] = octant % 2 + 2 * y_pos + 2 * SLAB_Y * z_pos
    meta[1:2, 0:parents] = dest_in[...] - (sp - 1) * slots

    @pl.when(has_next)
    def _():
        up_meta.start()

    @pl.when(has_prev)
    def _():
        dn_meta.start()

    for load in loads[0:2]:
        load.wait()
    raw = nbr[...]
    loc = jnp.where(raw >= 0, raw - bricks * (sp - 1), -FAR)
    here = iota((bricks, 1), 0) + bricks

    def loc_of(a, b, c):
        k = 9 * (a + 1) + tap2(b, c)
        if k == 13:
            return here
        k = k - (k > 13)
        return loc[:, k : k + 1]

    def place(a, first, sources, planes):
        wide_k = sources.shape[0]
        col = iota((bricks, wide_k), 1)
        keys = {
            (b, c): jnp.broadcast_to((loc_of(a, b, c) - first) * FACE, (bricks, wide_k))
            for b in (-1, 0, 1)
            for c in (-1, 0, 1)
        }
        for zq in range(PAD):
            c, sz = source(zq)
            hots = []
            for yq in range(PAD):
                b, sy = source(yq)
                hots.append(one(col == keys[b, c] + (sy * EDGE + sz)))
            placed = pick(jnp.concatenate(hots, axis=0), sources).astype(BF)
            for i, xq in enumerate(planes):
                pbuf[xq, :, :, zq * fine : (zq + 1) * fine] = placed[:, i * fine : (i + 1) * fine].reshape(
                    PAD, bricks, fine
                )

    def plane(i):
        return feat[:, i * FACE : (i + 1) * FACE, :].reshape(bricks * FACE, fine)

    place(0, bricks, jnp.concatenate([plane(i) for i in range(EDGE)], axis=1), range(1, EDGE + 1))
    place(-1, bricks, plane(EDGE - 1), [0])
    place(1, bricks, plane(0), [EDGE + 1])

    loads[5].wait()
    for z in range(EDGE):
        for bc in range(TAPS2):
            at = bc * reach + z * fine
            wt[z * wide : (z + 1) * wide, at : at + 3 * fine] = wf[:, bc * 3 * fine : (bc + 1) * 3 * fine]

    def cube(x, b):
        return pbuf[x, b : b + EDGE].reshape(line, reach)

    parts = []
    for a in range(3):
        for b in range(3):
            parts.append(jnp.concatenate([cube(x + a, b) for x in range(EDGE)], axis=0))
    total = lax.dot_general(jnp.concatenate(parts, axis=1), wt[...], NT, preferred_element_type=F32)
    part_h[0] = total[0:line]
    part_h[1] = total[(EDGE - 1) * line :]
    for x in range(1, EDGE - 1):
        g_buf[me, x + 1] = jnp.maximum(total[x * line : (x + 1) * line], 0.0).astype(BF)

    def rest(a, xq):
        taps = wt[:, (a + 1) * 3 * reach : (a + 2) * 3 * reach]
        return lax.dot_general(
            jnp.concatenate([cube(xq, b) for b in range(3)], axis=1), taps, NT, preferred_element_type=F32
        )

    spans = ((2, EDGE - 2), (EDGE, 1), (1, 1))

    def hid_copy(j, k, chan):
        ref = g_buf.at[me, pl.ds(*spans[j])]
        return rc(ref, ref, s2.at[j, k], r2.at[j, me], sp, chan)

    def hid_wait(j):
        for k in range(1, n_chan):
            src = lax.rem(me + k, n_chan)
            ref = g_buf.at[src, pl.ds(*spans[j])]
            rc(ref, ref, s2.at[j, 0], r2.at[j, src], sp, src).wait_recv()

    for k, chan in enumerate(peers):
        hid_copy(0, k, chan).start()

    @pl.when(has_next)
    def _():
        dn_feat.wait_recv()

    @pl.when(has_prev)
    def _():
        up_feat.wait_recv()

    place(1, 2 * bricks, fh[1].reshape(bricks * FACE, fine), [EDGE + 1])
    g_buf[me, EDGE] = jnp.maximum(part_h[1] + rest(1, EDGE + 1), 0.0).astype(BF)
    for k, chan in enumerate(peers):
        hid_copy(1, k, chan).start()

    twin = me + 1 - 2 * lax.rem(me, 2)
    spread_to = [lax.rem(c + 2 * j, n_chan) for j in range(n_chan // 2) for c in (me, twin)]

    def hid_halo(k):
        return rc(g_buf.at[me, EDGE], g_buf.at[me, 0], hs2.at[k], hr2.at[me], sp + 1, spread_to[k])

    @pl.when(has_next)
    def _():
        for k in range(n_chan):
            hid_halo(k).start()

    place(-1, 0, fh[0].reshape(bricks * FACE, fine), [0])
    g_buf[me, 1] = jnp.maximum(part_h[0] + rest(-1, 0), 0.0).astype(BF)
    for k, chan in enumerate(peers):
        hid_copy(2, k, chan).start()

    @pl.when(has_next)
    def _():
        dn_meta.wait_recv()

    @pl.when(has_prev)
    def _():
        up_meta.wait_recv()

    lanes = meta.shape[1]
    lane_par = jnp.where(
        iota((lanes, parents * cells), 1) % CLAYER // FACE == iota((lanes, parents * cells), 0), 1.0, 0.0
    )

    def dest_table(k):
        block = meta[...] if k == 1 else mh[k // 2]
        rel = jnp.dot(block.astype(F32), lane_par, preferred_element_type=F32)[1:2].astype(jnp.int32)
        slot = rel - (2 - k) * slots
        at = iota((1, parents * cells), 1)
        row = at % (HALF * CLAYER)
        target = slot * cells + (2 * (row // CLAYER) + at // (HALF * CLAYER)) * FACE + at % FACE
        ids = iota((slots * cells, parents * cells), 0)
        ohd[k] = one(ids == jnp.where((slot >= 0) & (slot < slots), target, -1))

    n_hot = HALF * HALF * bricks
    spread = jnp.where(iota((lanes, n_hot), 1) % bricks == iota((lanes, n_hot), 0), 1.0, 0.0)

    def key_of(block):
        code = jnp.dot(block.astype(F32), spread, preferred_element_type=F32)[0:1].astype(jnp.int32)
        sub = iota((1, n_hot), 1) // bricks
        y = 2 * (code // 2 % SLAB_Y) + sub % HALF
        z = 2 * (code // (2 * SLAB_Y)) + sub // HALF
        return code % 2, y * CZ + z

    keys = [(mh[0], 1), (meta[...], 0), (meta[...], 1), (mh[1], 0)]
    keys = [jnp.where(x_bit == want, key, -1) for (x_bit, key), want in ((key_of(m), w) for m, w in keys)]
    at = iota((CLAYER, n_hot), 0)
    par, yz = at // FACE, at % FACE
    for bc in range(TAPS2):
        y = par // (SLAB_Z // 2) * EDGE + yz // EDGE + bc // 3 - 1
        z = par % (SLAB_Z // 2) * EDGE + yz % EDGE + bc % 3 - 1
        want = jnp.where((y >= 0) & (y < CY) & (z >= 0) & (z < CZ), y * CZ + z, FAR)
        for k in range(4):
            hot_e[k, bc * CLAYER : (bc + 1) * CLAYER] = one(want == keys[k])

    for k in range(3):
        dest_table(k)

    for load in loads[6:8]:
        load.wait()

    hid_wait(0)

    full = EDGE * fine
    tail = fine * (EDGE - 1)

    def unpack(at):
        joined = jnp.concatenate(
            [jnp.concatenate([g_buf[s, x] for s in range(n_chan)], axis=1) for x in at], axis=0
        )
        moved = pick(joined, perm[...]).astype(BF)
        return [moved[i * line : (i + 1) * line] for i in range(len(at))]

    def hot_rows(a, c, n):
        col = iota((bricks, n), 1)
        rows = []
        for yq in range(LOW):
            b, sy = source(yq)
            where = loc_of(a, b, c)
            where = jnp.where(where >= bricks, where - bricks, where + line) + sy * bricks
            rows.append(one(col == where))
        return jnp.concatenate(rows, axis=0)

    def lay_out(at, moved):
        edge_y = pick(
            one(iota((bricks, bricks), 1) == loc_of(0, -1, 0) - bricks),
            jnp.concatenate([m[line - bricks :] for m in moved], axis=1),
        ).astype(BF)
        edge_z = pick(hot_rows(0, -1, line), jnp.concatenate([m[:, tail:] for m in moved], axis=1)).astype(BF)
        for i, x in enumerate(at):
            qbuf[x + 1, 1:LOW, :, fine : LOW * fine] = moved[i].reshape(EDGE, bricks, full)
            qbuf[x + 1, 0, :, fine : LOW * fine] = edge_y[:, i * full : (i + 1) * full]
            qbuf[x + 1, :, :, 0:fine] = edge_z[:, i * fine : (i + 1) * fine].reshape(LOW, bricks, fine)
    lay_out(list(range(1, EDGE - 1)), unpack(list(range(2, EDGE))))

    hid_wait(1)

    def down_taps(qx, taps):
        stacked = []
        for qz in range(HALF):
            for qy in range(HALF):
                stacked.append(
                    jnp.concatenate(
                        [
                            qbuf[2 * qx + a, 2 * qy + b, :, 2 * qz * fine : (2 * qz + 3) * fine]
                            for a in taps
                            for b in range(3)
                        ],
                        axis=1,
                    )
                )
        rows = jnp.concatenate(stacked, axis=0)
        at = taps[0] * TAPS2 * fine
        return lax.dot_general(rows, wd[:, at : at + rows.shape[1]], NT, preferred_element_type=F32)

    def down(qx, pieces):
        pieces = jnp.maximum(pieces, 0.0)
        c_buf[me, qx * side : (qx + 1) * side] = jnp.concatenate(
            [pieces[h * side : (h + 1) * side] for h in range(HALF)], axis=1
        ).astype(BF)

    def part_copy(qx, k, chan):
        ref = c_buf.at[me, pl.ds(qx * side, side)]
        return rc(ref, ref, s3.at[qx, k], r3.at[qx, me], sp, chan)

    def up_part(k):
        return rc(c_buf.at[me, pl.ds(side, side)], cp.at[me], hs3.at[0, k], hr3.at[0, me], sp + 1, spread_to[k])

    def dn_part(k):
        return rc(c_buf.at[me, pl.ds(0, side)], cn.at[me], hs3.at[1, k], hr3.at[1, me], sp - 1, spread_to[k])

    last = unpack([EDGE])
    lay_out([EDGE - 1], last)
    kept_row[...] = last[0]
    down(1, down_taps(1, range(3)))
    for k, chan in enumerate(peers):
        part_copy(1, k, chan).start()

    @pl.when(has_next)
    def _():
        for k in range(n_chan):
            up_part(k).start()

    hid_wait(2)
    lay_out([0], unpack([1]))
    base[...] = down_taps(0, range(1, 3))
    @pl.when(has_prev)
    def _():
        for chan in range(n_chan):
            rc(g_buf.at[chan, 0], g_buf.at[chan, 0], hs2.at[chan], hr2.at[chan], sp - 1, chan).wait_recv()

    joint = jnp.concatenate([kept_row[...], unpack([0])[0]], axis=0)
    qbuf[0, :, :, fine : LOW * fine] = pick(hot_rows(-1, 0, 2 * line), joint).astype(BF).reshape(LOW, bricks, full)
    qbuf[0, :, :, 0:fine] = pick(hot_rows(-1, -1, 2 * line), joint[:, tail:]).astype(BF).reshape(LOW, bricks, fine)
    down(0, base[...] + down_taps(0, range(1)))

    for k, chan in enumerate(peers):
        part_copy(0, k, chan).start()

    @pl.when(has_prev)
    def _():
        for k in range(n_chan):
            dn_part(k).start()

    for load in loads[8:]:
        load.wait()
    own = gain.shape[1]
    gain_col = jnp.sum(
        jnp.where(iota((own, own), 0) == iota((own, own), 1), gain[...], 0.0), axis=1, keepdims=True
    )

    def part_wait(qx):
        for k in range(1, n_chan):
            src = lax.rem(me + k, n_chan)
            ref = c_buf.at[src, pl.ds(qx * side, side)]
            rc(ref, ref, s3.at[qx, 0], r3.at[qx, src], sp, src).wait_recv()

    def all_channels(blocks):
        return jnp.concatenate(
            [
                jnp.concatenate([block[:, h * own_d : (h + 1) * own_d] for block in blocks], axis=1)
                for h in range(HALF)
            ],
            axis=0,
        )

    def fill(qx):
        inside = all_channels([c_buf[s, qx * side : (qx + 1) * side] for s in range(n_chan)])
        for x_bit in range(2):
            e_buf[2 * x_bit + qx + 1] = pick(hot_e[1 + x_bit], inside).astype(BF)

    span = TAPS2 * coarse

    def blocks(layers):
        return [
            jnp.concatenate([e_buf[x, bc * CLAYER : (bc + 1) * CLAYER] for x in layers], axis=0)
            for bc in range(TAPS2)
        ]

    def tap(a, layers):
        return lax.dot_general(
            wc[:, a * span : (a + 1) * span], jnp.concatenate(blocks(layers), axis=1), NT, preferred_element_type=F32
        )

    def pb_copy(side_k, h):
        step = 1 - 2 * side_k
        return rc(pb.at[1, h], pb.at[2 * side_k, h], s4.at[side_k, h], r4.at[side_k, h], sp + step, me)

    def settle(h, total):
        rounded = total.astype(BF)
        pb[1, h] = rounded
        values = rounded.astype(F32)
        pw[1, me, h] = jnp.sum(values * values, axis=0, keepdims=True)

        @pl.when(has_next)
        def _():
            pb_copy(0, h).start()

        @pl.when(has_prev)
        def _():
            pb_copy(1, h).start()

    part_wait(1)
    fill(1)
    acc[1] = tap(1, [2, 4])
    pair[0] = tap(2, [2, 4])
    single[0] = tap(0, [2])
    @pl.when(has_prev)
    def _():
        for chan in range(n_chan):
            rc(cp.at[chan], cp.at[chan], hs3.at[0, chan], hr3.at[0, chan], sp - 1, chan).wait_recv()

    e_buf[0] = pick(hot_e[0], all_channels([cp[s] for s in range(n_chan)])).astype(BF)
    acc[0] = pair[0] + jnp.concatenate([tap(0, [0]), single[0]], axis=1)
    part_wait(0)
    fill(0)
    acc[0] += tap(1, [1, 3])
    pair[1] = acc[1] + tap(0, [1, 3])
    single[1] = tap(2, [3])
    settle(0, acc[0])
    @pl.when(has_next)
    def _():
        for chan in range(n_chan):
            rc(cn.at[chan], cn.at[chan], hs3.at[1, chan], hr3.at[1, chan], sp + 1, chan).wait_recv()

    e_buf[CX + 1] = pick(hot_e[3], all_channels([cn[s] for s in range(n_chan)])).astype(BF)
    settle(1, pair[1] + jnp.concatenate([single[1], tap(2, [5])], axis=1))

    for k, chan in enumerate(peers):
        rc(pw.at[1, me], pw.at[1, me], ws4.at[1, k], wr4.at[1, me], sp, chan).start()

    @pl.when(has_next)
    def _():
        for k in range(n_chan):
            rc(pw.at[1, me], pw.at[0, me], ws4.at[0, k], wr4.at[0, me], sp + 1, spread_to[k]).start()

    @pl.when(has_prev)
    def _():
        for k in range(n_chan):
            rc(pw.at[1, me], pw.at[2, me], ws4.at[2, k], wr4.at[2, me], sp - 1, spread_to[k]).start()

    def normed(k):
        halves = []
        for h in range(HALF):
            power = pw[k, 0, h]
            for s in range(1, n_chan):
                power = power + pw[k, s, h]
            halves.append((pb[k, h].astype(F32) * lax.rsqrt(power / coarse + epsilon) * gain_col).astype(BF))
        return lax.dot_general(jnp.concatenate(halves, axis=1), ohd[k], NT, preferred_element_type=F32)

    for k in range(1, n_chan):
        src = lax.rem(me + k, n_chan)
        rc(pw.at[1, src], pw.at[1, src], ws4.at[1, 0], wr4.at[1, src], sp, src).wait_recv()
    kept[...] = normed(1)

    @pl.when(has_prev)
    def _():
        for h in range(HALF):
            pb_copy(0, h).wait_recv()
        for chan in range(n_chan):
            rc(pw.at[0, chan], pw.at[0, chan], ws4.at[0, chan], wr4.at[0, chan], sp - 1, chan).wait_recv()

    @pl.when(has_next)
    def _():
        for h in range(HALF):
            pb_copy(1, h).wait_recv()
        for chan in range(n_chan):
            rc(pw.at[2, chan], pw.at[2, chan], ws4.at[2, chan], wr4.at[2, chan], sp + 1, chan).wait_recv()

    out[...] = (kept[...] + normed(0) + normed(2)).astype(BF)

    for k, chan in enumerate(peers):
        for j in range(3):
            hid_copy(j, k, chan).wait_send()
        for qx in range(HALF):
            part_copy(qx, k, chan).wait_send()
        rc(pw.at[1, me], pw.at[1, me], ws4.at[1, k], wr4.at[1, me], sp, chan).wait_send()

    @pl.when(has_next)
    def _():
        up_meta.wait_send()
        up_feat.wait_send()
        for h in range(HALF):
            pb_copy(0, h).wait_send()
        for chan in range(n_chan):
            hid_halo(chan).wait_send()
            up_part(chan).wait_send()
            rc(pw.at[1, me], pw.at[0, me], ws4.at[0, chan], wr4.at[0, me], sp + 1, spread_to[chan]).wait_send()

    @pl.when(has_prev)
    def _():
        dn_meta.wait_send()
        dn_feat.wait_send()
        for h in range(HALF):
            pb_copy(1, h).wait_send()
        for chan in range(n_chan):
            dn_part(chan).wait_send()
            rc(pw.at[1, me], pw.at[2, me], ws4.at[2, chan], wr4.at[2, me], sp - 1, spread_to[chan]).wait_send()


def body(n_space, n_chan, features, neighbours, parent_index, octant, parent_dest, conv_fine, conv_down, conv_coarse, norm_gain):
    bricks, _, fine = features.shape
    parents = parent_dest.shape[0]
    slots = 2 * parents
    own_d = conv_down.shape[0]
    own = conv_coarse.shape[0]
    cells = EDGE**3
    coarse = own_d * n_chan
    group = EDGE * fine // n_chan
    vmem = pl.BlockSpec(memory_space=pltpu.VMEM)
    hbm = pl.BlockSpec(memory_space=pltpu.HBM)
    dma = pltpu.SemaphoreType.DMA

    def fixed(x):
        return pltpu.with_memory_space_constraint(x, pltpu.HBM)

    return pl.pallas_call(
        functools.partial(fused_kernel, n_space, n_chan, bricks, slots),
        out_shape=jax.ShapeDtypeStruct((own, slots * cells), BF),
        in_specs=[hbm] * 10,
        out_specs=vmem,
        scratch_shapes=[
            pltpu.VMEM(features.shape, BF),
            pltpu.VMEM(neighbours.shape, jnp.int32),
            pltpu.VMEM(conv_fine.shape, BF),
            pltpu.VMEM((group, TAPS2 * PAD * fine), BF),
            pltpu.VMEM((1, own), F32),
            pltpu.VMEM((1, bricks), jnp.int32),
            pltpu.VMEM((1, bricks), jnp.int32),
            pltpu.VMEM((1, parents), jnp.int32),
            pltpu.VMEM((8, 128), jnp.int32),
            pltpu.VMEM(conv_down.shape, BF),
            pltpu.VMEM(conv_coarse.shape, BF),
            pltpu.VMEM((n_chan * group, n_chan * group), BF),
            pltpu.VMEM((2, bricks, FACE, fine), BF),
            pltpu.VMEM((2, 8, 128), jnp.int32),
            pltpu.VMEM((PAD, PAD, bricks, PAD * fine), BF),
            pltpu.VMEM((2, EDGE * bricks, group), F32),
            pltpu.VMEM((n_chan, LOW, EDGE * bricks, group), BF),
            pltpu.VMEM((LOW, LOW, bricks, LOW * fine), BF),
            pltpu.VMEM((n_chan, HALF * HALF * bricks, HALF * own_d), BF),
            pltpu.VMEM((n_chan, HALF * bricks, HALF * own_d), BF),
            pltpu.VMEM((n_chan, HALF * bricks, HALF * own_d), BF),
            pltpu.VMEM((CX + 2, TAPS2 * CLAYER, coarse), BF),
            pltpu.VMEM((4, TAPS2 * CLAYER, HALF**2 * bricks), BF),
            pltpu.VMEM((HALF, own, HALF * CLAYER), F32),
            pltpu.VMEM((HALF, own, HALF * CLAYER), F32),
            pltpu.VMEM((HALF, own, CLAYER), F32),
            pltpu.VMEM((own, slots * cells), F32),
            pltpu.VMEM((EDGE * bricks, EDGE * fine), BF),
            pltpu.VMEM((HALF * HALF * bricks, own_d), F32),
            pltpu.VMEM((3, HALF, own, HALF * CLAYER), BF),
            pltpu.VMEM((3, n_chan, HALF, 1, HALF * CLAYER), F32),
            pltpu.VMEM((3, slots * cells, parents * cells), BF),
            dma((10,)),
            dma((2, 2)),
            dma((2, 2)),
            dma((3, n_chan - 1)),
            dma((3, n_chan)),
            dma((n_chan,)),
            dma((n_chan,)),
            dma((HALF, n_chan - 1)),
            dma((HALF, n_chan)),
            dma((2, n_chan)),
            dma((2, n_chan)),
            dma((2, HALF)),
            dma((2, HALF)),
            dma((3, n_chan)),
            dma((3, n_chan)),
        ],
        compiler_params=pltpu.CompilerParams(
            collective_id=0, has_side_effects=True, vmem_limit_bytes=40000000
        ),
    )(
        fixed(features),
        fixed(neighbours),
        fixed(parent_index.reshape(1, -1)),
        fixed(octant.reshape(1, -1)),
        fixed(parent_dest.reshape(1, -1)),
        fixed(conv_fine),
        fixed(conv_down),
        fixed(conv_coarse),
        fixed(norm_gain.reshape(1, -1)),
        fixed(table(n_chan, fine)),
    )


def solution(mesh):
    sizes = dict(mesh.shape)
    return jax.shard_map(
        functools.partial(body, sizes["space"], sizes["chan"]),
        mesh=mesh,
        in_specs=(
            P("space", None, None),
            P("space", None),
            P("space"),
            P("space"),
            P("space"),
            P("chan", None),
            P("chan", None),
            P("chan", None),
            P("chan"),
        ),
        out_specs=P("chan", "space"),
        check_vma=False,
    )
```
